128 devices in a mesh: row: 8 (over z, core), col: 16 (over y, x).
Axes of the slice: x: 4, y: 4, z: 4, core: 2. Of those that a mesh axis runs over, the one named last changes fastest.
Arguments:
- emb: bfloat16 [524288, 512], P(('row', 'col')), may hold values from -6 to 6
- tiles: bfloat16 [2048, 4, 256, 256], P(('row', 'col')), may hold values from -0.375 to 0.375
- msg_src: int32 [2048, 4], P(('row', 'col')), may hold values from 0 to 15
- msg_dst: int32 [2048, 4], P(('row', 'col')), may hold values from 0 to 16, as said below
- msg_count: int32 [2048, 4], P(('row', 'col')), may hold values from 1 to 256
- weight: bfloat16 [512, 512], replicated, may hold values from -0.25 to 0.25
- docs: bfloat16 [512, 512], P('row'), may hold values from -0.059814453 to 0.099609375
- doc_labels: int32 [512, 8], replicated, may hold values from 0 to 524287
Outputs:
- hidden: bfloat16 [524288, 512], P(('row', 'col'))
- grad_docs: float32 [512, 512], P('row')
- grad_weight: float32 [512, 512], replicated
The draws below stay inside these ranges and needn't reach their ends.
Inputs may be any that keep to these rules, and one draw needn't show every extreme that they name: For each sending device and each column of its row, the used slots (msg_dst below 16) come first and 16 marks an unused slot. In every row of devices some column receives all 4 slots used from every sender of that row.
All inputs are finite; a program needn't handle non-finite values.
Results may differ from the reference program's by a relative error of at most 0.0052.
Values may be sent and summed in bfloat16 or wider, within the bound.
No kernel may reach another device: no remote copies, remote signals or barrier semaphores. Data moves between devices by JAX's collectives and lax.ppermute only.
A program may use at most 192 MiB of HBM per device.

```python
import jax
import jax.numpy as jnp
from jax import lax

D = 512
LABEL_DEV = 4096
BLK = 256
CAP = 4
POS = 8
BLK_DEV = 16
LABELS = 524288
DOCS = 512
N_ROW = 8
N_COL = 16


def draw_msg_dst(key, part):
    rows = N_ROW * N_COL * N_COL
    index = jnp.arange(rows, dtype=jnp.int32)
    sender = index // N_COL
    peer = index % N_COL
    row_of = sender // N_COL
    heavy = jax.random.randint(jax.random.fold_in(key, 11), (N_ROW * N_COL,), 0, 4) == 0
    light = jax.random.randint(jax.random.fold_in(key, 12), (rows,), 0, CAP // 2 + 1)
    full_col = jax.random.randint(jax.random.fold_in(key, 13), (N_ROW,), 0, N_COL)
    filled = jnp.where(heavy[sender] | (peer == full_col[row_of]), CAP, light)
    slot_ids = jnp.arange(CAP, dtype=jnp.int32)
    chosen = jax.random.randint(jax.random.fold_in(key, 14), (rows, CAP), 0, BLK_DEV)
    return jnp.where(slot_ids[None, :] < filled[:, None], chosen, BLK_DEV).astype(jnp.int32)


def with_ends(entries, rng, least, largest):
    place = [jax.random.randint(jax.random.fold_in(rng, axis), (), 0, length) for axis, length in enumerate(entries.shape)]
    widest = entries.shape.index(max(entries.shape))
    neighbour = place[:widest] + [(place[widest] + 1) % entries.shape[widest]] + place[widest + 1:]
    return entries.at[tuple(place)].set(least).at[tuple(neighbour)].set(largest)


def shard_levels(rng, shape, split, least, top_value):
    def one(dim, shards_of):
        heights = jax.random.uniform(jax.random.fold_in(jax.random.fold_in(rng, 6), dim), (shards_of,), jnp.float32, least / len(split), top_value / len(split))
        return jnp.repeat(jnp.exp(heights), shape[dim] // shards_of).reshape((-1,) + (1,) * (len(shape) - dim - 1))

    factor_of = one(*split[0])
    for cut in split[1:]:
        factor_of = factor_of * one(*cut)
    return factor_of


def centred(stream_key, extent, scale, most, split=(), kind=jnp.bfloat16):
    drawn = scale * jax.random.normal(stream_key, extent, jnp.float32)
    if split:
        drawn = drawn * shard_levels(stream_key, extent, split, -0.22, 0.18)
    return jnp.clip(drawn, -most, most).astype(kind)


def setup_inputs(seed: int = 0) -> dict:
    keys = jax.random.split(jax.random.key(seed), 9)
    return {
        "emb": centred(keys[0], (LABELS, D), 1.0, 6.0, ((0, 128),)),
        "tiles": centred(keys[1], (N_ROW * N_COL * N_COL, CAP, BLK, BLK), BLK ** -0.5, 0.375, ((0, 128),)),
        "msg_src": with_ends(jax.random.randint(keys[2], (N_ROW * N_COL * N_COL, CAP), 0, BLK_DEV), jax.random.fold_in(keys[2], 1), 0, BLK_DEV - 1).astype(jnp.int32),
        "msg_dst": draw_msg_dst(jax.random.fold_in(keys[8], 71), 0),
        "msg_count": with_ends(jax.random.randint(keys[4], (N_ROW * N_COL * N_COL, CAP), 1, BLK + 1), jax.random.fold_in(keys[4], 1), 1, BLK).astype(jnp.int32),
        "weight": centred(keys[5], (D, D), D ** -0.5, 0.25),
        "docs": jnp.clip(-0.059814453 + 0.15942383 * jax.random.uniform(keys[6], (DOCS, D), jnp.float32) ** shard_levels(keys[6], (DOCS, D), ((0, 8),), -0.2, 0.2), -0.059814453, 0.099609375).astype(jnp.bfloat16),
        "doc_labels": with_ends(jax.random.randint(keys[7], (DOCS, POS), 0, LABELS), jax.random.fold_in(keys[7], 1), 0, LABELS - 1).astype(jnp.int32),
    }


def reference(emb, tiles, msg_src, msg_dst, msg_count, weight, docs, doc_labels):
    n_dev = N_ROW * N_COL
    blocks = emb.reshape(n_dev, BLK_DEV, BLK, D)
    src_all = msg_src.reshape(n_dev, N_COL, CAP)
    dst_all = msg_dst.reshape(n_dev, N_COL, CAP)
    cnt_all = msg_count.reshape(n_dev, N_COL, CAP)
    tile_all = tiles.reshape(n_dev, N_COL, CAP, BLK, BLK)
    labels_total = float(LABEL_DEV * n_dev)
    block_ids = jnp.arange(BLK_DEV, dtype=jnp.int32)

    def one_device(carry, device):
        doc_sum, weight_sum = carry
        row_index = device // N_COL
        col_index = device % N_COL
        senders = row_index * N_COL + jnp.arange(N_COL, dtype=jnp.int32)
        source = src_all[senders, col_index]
        target = dst_all[senders, col_index]
        counts = cnt_all[senders, col_index].astype(jnp.float32)
        tile_set = tile_all[senders, col_index]
        picked = blocks[senders[:, None], source]
        messages = jnp.einsum("pqij,pqjd->pqid", tile_set.astype(jnp.float32),
                              picked.astype(jnp.float32)).astype(jnp.bfloat16)
        hot = (target[None, :, :] == block_ids[:, None, None]).astype(jnp.float32)
        weighted = hot * counts[None]
        total = jnp.einsum("bpq,pqid->bid", weighted, messages.astype(jnp.float32))
        total = total + float(BLK) * blocks[device].astype(jnp.float32)
        denom = float(BLK) + jnp.sum(weighted, axis=(1, 2))
        agg = (total / denom[:, None, None]).astype(jnp.bfloat16).reshape(LABEL_DEV, D)
        pre = jnp.dot(agg, weight, preferred_element_type=jnp.float32)
        hidden = jax.nn.silu(pre).astype(jnp.bfloat16)
        scores = jnp.dot(docs, hidden.T, preferred_element_type=jnp.float32)
        label_ids = device * LABEL_DEV + jnp.arange(LABEL_DEV, dtype=jnp.int32)
        positive = jnp.any(doc_labels[:, :, None] == label_ids[None, None, :], axis=1)
        prob = jax.nn.sigmoid(scores)
        dscore = jnp.where(positive, (prob - 1.0) / float(POS), prob / labels_total).astype(jnp.bfloat16)
        doc_part = jnp.dot(dscore, hidden, preferred_element_type=jnp.float32)
        dhid = jnp.dot(dscore.T, docs, preferred_element_type=jnp.float32)
        sig = jax.nn.sigmoid(pre)
        dpre = (dhid * sig * (1.0 + pre * (1.0 - sig))).astype(jnp.bfloat16)
        weight_part = jnp.dot(agg.T, dpre, preferred_element_type=jnp.float32)
        return (doc_sum + doc_part, weight_sum + weight_part), hidden

    start = (jnp.zeros((DOCS, D), jnp.float32), jnp.zeros((D, D), jnp.float32))
    (grad_docs, grad_weight), hiddens = lax.scan(one_device, start, jnp.arange(n_dev, dtype=jnp.int32))
    return hiddens.reshape(LABELS, D), grad_docs, grad_weight
```

```python
import jax
import jax.numpy as jnp
from jax import lax
from jax.experimental import pallas as pl
from jax.experimental.pallas import tpu as pltpu
from jax.sharding import PartitionSpec as P

BF = jnp.bfloat16
F32 = jnp.float32
CHUNK_ROWS = (64, 64, 64, 64)
STEP_ROWS = 32


def message_kernel(src_ref, emb_ref, tile_ref, out_ref):
    p = pl.program_id(0)
    for q in range(tile_ref.shape[1]):
        block = emb_ref[src_ref[p, q]]
        out_ref[0, q] = jnp.dot(
            tile_ref[0, q], block, preferred_element_type=F32
        ).astype(BF)


def messages_of(src, blocks, tiles, row, rows):
    n_peer, cap, blk, _ = tiles.shape
    n_blk, _, width = blocks.shape
    at = row // rows
    return pl.pallas_call(
        message_kernel,
        grid_spec=pltpu.PrefetchScalarGridSpec(
            num_scalar_prefetch=1,
            grid=(n_peer,),
            in_specs=[
                pl.BlockSpec((n_blk, blk, width), lambda p, s: (0, 0, 0),
                             pipeline_mode=pl.Buffered(1)),
                pl.BlockSpec((1, cap, rows, blk), lambda p, s: (p, 0, at, 0)),
            ],
            out_specs=pl.BlockSpec((1, cap, rows, width), lambda p, s: (p, 0, 0, 0)),
        ),
        out_shape=jax.ShapeDtypeStruct((n_peer, cap, rows, width), BF),
        name="messages",
    )(src, blocks, tiles)


def head_kernel(first, blk, labels_total, pos_count,
                dst_ref, cnt_ref, inv_ref, recv_ref, emb_ref, pos_ref, w_ref, docs_ref,
                *rest):
    if first:
        hid_ref, gd_ref, gw_ref, acc_ref, agg_ref, ds_ref = rest
    else:
        gd_in, gw_in, _, hid_ref, gd_ref, gw_ref, acc_ref, agg_ref, ds_ref = rest
    step = pl.program_id(0)

    @pl.when(step == 0)
    def _():
        if first:
            gd_ref[...] = jnp.zeros_like(gd_ref)
            gw_ref[...] = jnp.zeros_like(gw_ref)
        else:
            gd_ref[...] = gd_in[...]
            gw_ref[...] = gw_in[...]

    n_blk, rows, width = emb_ref.shape
    own = float(blk)
    for b in range(n_blk):
        acc_ref[b] = own * emb_ref[b].astype(F32)
    n_slot = recv_ref.shape[0]

    def add(s, carry):
        d = dst_ref[s]

        @pl.when(d < n_blk)
        def _():
            acc_ref[d] = acc_ref[d] + cnt_ref[s] * recv_ref[s].astype(F32)
        return carry

    lax.fori_loop(0, n_slot, add, 0)
    for b in range(n_blk):
        agg_ref[b * rows:(b + 1) * rows, :] = (acc_ref[b] * inv_ref[b]).astype(BF)
    agg = agg_ref[...]
    pre = jnp.dot(agg, w_ref[...], preferred_element_type=F32)
    sig = 1.0 / (1.0 + jnp.exp(-pre))
    hid = (pre * sig).astype(BF)
    for b in range(n_blk):
        hid_ref[b] = hid[b * rows:(b + 1) * rows, :]
    scores = lax.dot_general(hid, docs_ref[...], (((1,), (1,)), ((), ())),
                             preferred_element_type=F32)
    prob = 1.0 / (1.0 + jnp.exp(-scores))
    for b in range(n_blk):
        part = prob[b * rows:(b + 1) * rows, :]
        ds_ref[b * rows:(b + 1) * rows, :] = jnp.where(
            pos_ref[b].astype(F32) > 0.5, (part - 1.0) * (1.0 / pos_count), part * (1.0 / labels_total)
        ).astype(BF)
    ds = ds_ref[...]
    gd_ref[...] += lax.dot_general(ds, hid, (((0,), (0,)), ((), ())),
                                   preferred_element_type=F32)
    dhid = jnp.dot(ds, docs_ref[...], preferred_element_type=F32)
    dpre = (dhid * sig * (1.0 + pre * (1.0 - sig))).astype(BF)
    gw_ref[...] += lax.dot_general(agg, dpre, (((0,), (0,)), ((), ())),
                                   preferred_element_type=F32)


def head(dst, cnt, inv, recv, blocks, positive, weight, docs, carry, row, rows,
         labels_total, pos_count):
    n_blk, blk, width = blocks.shape
    n_slot = recv.shape[0]
    step_rows = min(STEP_ROWS, rows)
    steps = rows // step_rows
    at = row // step_rows
    n_doc = docs.shape[0]
    first = carry is None
    smem = pl.BlockSpec(memory_space=pltpu.SMEM)
    full = lambda a: pl.BlockSpec(a, lambda i: (0, 0), pipeline_mode=pl.Buffered(1))
    rowed = lambda n: pl.BlockSpec((n_blk, step_rows, n), lambda i: (0, at + i, 0))
    in_specs = [
        smem, smem, smem,
        pl.BlockSpec((n_slot, step_rows, width), lambda i: (0, i, 0)),
        rowed(width), rowed(n_doc), full(weight.shape), full(docs.shape),
    ]
    args = [dst, cnt, inv, recv, blocks, positive, weight, docs]
    aliases = {}
    if not first:
        hid, gd, gw = carry
        in_specs += [full(gd.shape), full(gw.shape), pl.BlockSpec(memory_space=pl.ANY)]
        aliases = {len(args) + 2: 0}
        args += [gd, gw, hid]

    def body(*refs):
        head_kernel(first, blk, labels_total, pos_count, *refs)

    return pl.pallas_call(
        body,
        grid=(steps,),
        in_specs=in_specs,
        out_specs=[rowed(width),
                   pl.BlockSpec((n_doc, width), lambda i: (0, 0)),
                   pl.BlockSpec((width, width), lambda i: (0, 0))],
        out_shape=[jax.ShapeDtypeStruct(blocks.shape, BF),
                   jax.ShapeDtypeStruct((n_doc, width), F32),
                   jax.ShapeDtypeStruct((width, width), F32)],
        scratch_shapes=[pltpu.VMEM((n_blk, step_rows, width), F32),
                        pltpu.VMEM((n_blk * step_rows, width), BF),
                        pltpu.VMEM((n_blk * step_rows, n_doc), BF)],
        input_output_aliases=aliases,
        compiler_params=pltpu.CompilerParams(vmem_limit_bytes=48 << 20),
        name="head",
    )(*args)


def swap(x, axis):
    return lax.all_to_all(x, axis, split_axis=0, concat_axis=0, tiled=True)


def spread(x, axis, n):
    return swap(jnp.broadcast_to(x[None], (n,) + x.shape), axis)


def per_device(emb, tiles, msg_src, msg_dst, msg_count, weight, docs, doc_labels):
    n_col = lax.axis_size("col")
    n_row = lax.axis_size("row")
    label_dev, width = emb.shape
    n_peer, cap, blk, _ = tiles.shape
    blk_dev = label_dev // blk
    labels_total = float(label_dev * n_row * n_col)
    pos_count = doc_labels.shape[1]
    n_doc = docs.shape[0] * n_row
    blocks = emb.reshape(blk_dev, blk, width)

    starts = [sum(CHUNK_ROWS[:k]) for k in range(len(CHUNK_ROWS))]
    received = []
    sent = []
    for row, rows in zip(starts, CHUNK_ROWS):
        out = messages_of(msg_src, blocks, tiles, row, rows)
        sent.append(out)
        received.append(swap(out, "col").reshape(n_peer * cap, rows, width))

    table = swap(jnp.concatenate([msg_dst, msg_count], axis=1), "col")
    dst = table[:, :cap].reshape(-1)
    cnt = table[:, cap:].reshape(-1).astype(F32)
    hot = dst[None, :] == jnp.arange(blk_dev, dtype=jnp.int32)[:, None]
    inv = 1.0 / (float(blk) + jnp.sum(jnp.where(hot, cnt[None, :], 0.0), axis=1))

    all_docs = spread(docs, "row", n_row).reshape(n_doc, width)
    device = lax.axis_index("row") * n_col + lax.axis_index("col")
    label_ids = device * label_dev + jnp.arange(label_dev, dtype=jnp.int32)
    positive = jnp.any(
        label_ids[:, None, None] == doc_labels.T[None, :, :], axis=1
    ).astype(BF).reshape(blk_dev, blk, n_doc)

    carry = None
    for k, (row, rows) in enumerate(zip(starts, CHUNK_ROWS)):
        carry = head(dst, cnt, inv, received[k], blocks, positive, weight, all_docs, carry,
                     row, rows, labels_total, float(pos_count))
    hidden, gd, gw = carry

    both = jnp.concatenate([gd, gw], axis=1).astype(BF)
    share = n_doc // n_col
    part = swap(both.reshape(n_col, share, 2 * width), "col")
    part = jnp.sum(part.astype(F32), axis=0).astype(BF)
    part = spread(part, "row", n_row)
    part = jnp.sum(part.astype(F32), axis=0).astype(BF)
    whole = spread(part, "col", n_col).reshape(n_doc, 2 * width)
    mine = lax.dynamic_slice_in_dim(
        whole[:, :width], lax.axis_index("row") * docs.shape[0], docs.shape[0], 0
    )
    return (hidden.reshape(label_dev, width), mine.astype(F32), whole[:, width:].astype(F32))


def solution(mesh):
    in_specs = (
        P(("row", "col"), None),
        P(("row", "col"), None, None, None),
        P(("row", "col"), None),
        P(("row", "col"), None),
        P(("row", "col"), None),
        P(),
        P("row", None),
        P(),
    )
    out_specs = (P(("row", "col"), None), P("row", None), P())
    return jax.shard_map(
        per_device, mesh=mesh, in_specs=in_specs, out_specs=out_specs, check_vma=False
    )
```

```python
import functools

import jax
import jax.numpy as jnp
from jax import lax
from jax.experimental import pallas as pl
from jax.experimental.pallas import tpu as pltpu
from jax.sharding import PartitionSpec as P

BF = jnp.bfloat16
F32 = jnp.float32
CHUNK_ROWS = (128, 128)
STEP_ROWS = 32
RING = 4


def hbm(v):
    return pltpu.with_memory_space_constraint(v, pltpu.HBM)


def wrap(i):
    return lax.rem(i + RING, RING)


def shift_pairs(axis, by):
    pairs = []
    for y in range(RING):
        for x in range(RING):
            ty, tx = ((y + by) % RING, x) if axis == "y" else (y, (x + by) % RING)
            pairs.append((y * RING + x, ty * RING + tx))
    return pairs


def shift(v, axis, by):
    return hbm(lax.ppermute(v, "col", shift_pairs(axis, by)))


def message_kernel(order_ref, src_ref, emb_ref, *refs):
    d = pl.program_id(0)
    for j in range(RING):
        tile_ref, out_ref = refs[j], refs[RING + j]
        p = order_ref[j * RING + d]
        for q in range(tile_ref.shape[1]):
            out_ref[0, q] = jnp.dot(
                tile_ref[0, q], emb_ref[src_ref[p, q]], preferred_element_type=F32
            ).astype(BF)


def messages_of(order, src, blocks, tiles, row, rows, half):
    n_peer, cap, blk, _ = tiles.shape
    n_blk, _, width = blocks.shape
    at = row // rows
    part = width // 2
    shape = (RING, cap, rows, part)
    return pl.pallas_call(
        message_kernel,
        grid_spec=pltpu.PrefetchScalarGridSpec(
            num_scalar_prefetch=2,
            grid=(RING,),
            in_specs=[
                pl.BlockSpec((n_blk, blk, part), lambda i, o, s: (0, 0, half),
                             pipeline_mode=pl.Buffered(1)),
            ] + [
                pl.BlockSpec((1, cap, rows, blk),
                             lambda i, o, s, j=j: (o[j * RING + i], 0, at, 0))
                for j in range(RING)
            ],
            out_specs=[pl.BlockSpec((1,) + shape[1:], lambda i, o, s: (i, 0, 0, 0))] * RING,
        ),
        out_shape=[jax.ShapeDtypeStruct(shape, BF)] * RING,
        name=f"messages_{row}_{half}",
    )(order, src, blocks, *[tiles] * RING)


def add_slots(acc_ref, table_ref, y, x, half, ahead, parts, columns):
    n_blk = acc_ref.shape[0]
    cap = parts[0].shape[1]
    for came, ref in enumerate(parts):
        if half == 0:
            s = y * RING + wrap(x - came)
            p = wrap(y + ahead) * RING + x
        else:
            s = wrap(y - came) * RING + x
            p = y * RING + wrap(x + ahead)
        def add(q, carry):
            dst = table_ref[s, p * 2 * cap + q]
            cnt = table_ref[s, p * 2 * cap + cap + q].astype(F32)

            @pl.when(dst < n_blk)
            def _():
                acc_ref[dst, :, columns] = (
                    acc_ref[dst, :, columns] + cnt * ref[0, q].astype(F32)
                )
            return carry

        lax.fori_loop(0, cap, add, 0)


def far_kernel(half, pos_ref, table_ref, *refs):
    parts, (low_ref, high_ref, acc_ref) = refs[:RING], refs[-3:]
    acc_ref[...] = jnp.zeros_like(acc_ref)
    add_slots(acc_ref, table_ref, pos_ref[0], pos_ref[1], half, 2, parts, slice(None))
    n = low_ref.shape[0]
    low_ref[...] = acc_ref[:n].astype(BF)
    high_ref[...] = acc_ref[n:].astype(BF)


def near_kernel(half, pos_ref, table_ref, *refs):
    ones, threes = refs[:RING], refs[RING:2 * RING]
    low_in, high_in, up_ref, down_ref, acc_ref = refs[2 * RING:]
    n = low_in.shape[0]
    acc_ref[:n] = low_in[...].astype(F32)
    acc_ref[n:] = jnp.zeros_like(acc_ref[n:])
    add_slots(acc_ref, table_ref, pos_ref[0], pos_ref[1], half, 1, ones, slice(None))
    up_ref[...] = acc_ref[...].astype(BF)
    acc_ref[:n] = jnp.zeros_like(acc_ref[:n])
    acc_ref[n:] = high_in[...].astype(F32)
    add_slots(acc_ref, table_ref, pos_ref[0], pos_ref[1], half, 3, threes, slice(None))
    down_ref[...] = acc_ref[...].astype(BF)


SMEM = pl.BlockSpec(memory_space=pltpu.SMEM)


def slot_spec(part, step_rows, ahead):
    return pl.BlockSpec((1, part.shape[1], step_rows, part.shape[3]),
                        lambda i: (ahead, 0, i, 0))


def far_sums(half, pos, table, parts, n_blk, after):
    _, _, rows, cols = parts[0].shape
    step_rows = min(STEP_ROWS, rows)
    n = n_blk // 2
    return pl.pallas_call(
        functools.partial(far_kernel, half),
        grid=(rows // step_rows,),
        in_specs=[SMEM, SMEM] + [slot_spec(a, step_rows, 2) for a in parts]
        + [pl.BlockSpec(memory_space=pl.ANY)] * len(after),
        out_specs=[pl.BlockSpec((n, step_rows, cols), lambda i: (0, i, 0))] * 2,
        out_shape=[jax.ShapeDtypeStruct((n, rows, cols), BF)] * 2,
        scratch_shapes=[pltpu.VMEM((n_blk, step_rows, cols), F32)],
        name=f"far_{half}",
    )(pos, table, *parts, *after)


def near_sums(half, pos, table, parts, low, high):
    _, _, rows, cols = parts[0].shape
    step_rows = min(STEP_ROWS, rows)
    n = low.shape[0]
    rowed = lambda k: pl.BlockSpec((k, step_rows, cols), lambda i: (0, i, 0))
    return pl.pallas_call(
        functools.partial(near_kernel, half),
        grid=(rows // step_rows,),
        in_specs=[SMEM, SMEM] + [slot_spec(a, step_rows, 1) for a in parts]
        + [slot_spec(a, step_rows, 3) for a in parts] + [rowed(n), rowed(n)],
        out_specs=[rowed(2 * n)] * 2,
        out_shape=[jax.ShapeDtypeStruct((2 * n, rows, cols), BF)] * 2,
        scratch_shapes=[pltpu.VMEM((2 * n, step_rows, cols), F32)],
        name=f"near_{half}",
    )(pos, table, *parts, *parts, low, high)


def head_kernel(first, row, blk, labels_total, pos_count,
                pos_ref, table_ref, inv_ref, near_ref, *refs):
    mine = (refs[:RING], refs[RING:2 * RING])
    refs = refs[2 * RING:]
    sums = (refs[:2], refs[2:4])
    emb_ref, labels_ref, w_ref, docs_ref = refs[4:8]
    rest = refs[8:]
    if first:
        hid_ref, gd_ref, gw_ref, acc_ref, agg_ref, ds_ref = rest
    else:
        gd_in, gw_in, _, hid_ref, gd_ref, gw_ref, acc_ref, agg_ref, ds_ref = rest
    step = pl.program_id(0)

    @pl.when(step == 0)
    def _():
        if first:
            gd_ref[...] = jnp.zeros_like(gd_ref)
            gw_ref[...] = jnp.zeros_like(gw_ref)
        else:
            gd_ref[...] = gd_in[...]
            gw_ref[...] = gw_in[...]

    n_blk, rows, width = emb_ref.shape
    part = width // 2
    for half in range(2):
        columns = slice(half * part, (half + 1) * part)
        up, down = sums[half]
        for b in range(n_blk):
            acc_ref[b, :, columns] = (
                float(blk) * emb_ref[b, :, columns].astype(F32)
                + up[b].astype(F32) + down[b].astype(F32)
            )
        add_slots(acc_ref, table_ref, pos_ref[0], pos_ref[1], half, 0, mine[half], columns)
    for b in range(n_blk):
        agg_ref[b * rows:(b + 1) * rows, :] = (acc_ref[b] * inv_ref[b]).astype(BF)
    agg = agg_ref[...]
    pre = jnp.dot(agg, w_ref[...], preferred_element_type=F32)
    sig = 1.0 / (1.0 + jnp.exp(-pre))
    hid = (pre * sig).astype(BF)
    for b in range(n_blk):
        hid_ref[b] = hid[b * rows:(b + 1) * rows, :]
    scores = lax.dot_general(hid, docs_ref[...], (((1,), (1,)), ((), ())),
                             preferred_element_type=F32)
    prob = 1.0 / (1.0 + jnp.exp(-scores))
    for b in range(n_blk):
        one = prob[b * rows:(b + 1) * rows, :]
        ds_ref[b * rows:(b + 1) * rows, :] = (one * (1.0 / labels_total)).astype(BF)

        @pl.when(near_ref[(b * blk + row) // rows + step] > 0)
        def _():
            ids = b * blk + row + step * rows + lax.broadcasted_iota(jnp.int32, one.shape, 0)
            hit = labels_ref[0:1, :] == ids
            for j in range(1, labels_ref.shape[0]):
                hit = hit | (labels_ref[j:j + 1, :] == ids)
            ds_ref[b * rows:(b + 1) * rows, :] = jnp.where(
                hit, (one - 1.0) * (1.0 / pos_count), one * (1.0 / labels_total)
            ).astype(BF)
    ds = ds_ref[...]
    gd_ref[...] += lax.dot_general(ds, hid, (((0,), (0,)), ((), ())),
                                   preferred_element_type=F32)
    dhid = jnp.dot(ds, docs_ref[...], preferred_element_type=F32)
    dpre = (dhid * sig * (1.0 + pre * (1.0 - sig))).astype(BF)
    gw_ref[...] += lax.dot_general(agg, dpre, (((0,), (0,)), ((), ())),
                                   preferred_element_type=F32)


def head(pos, table, inv, near, mine, sums, blocks, labels, weight, docs, carry, row,
         labels_total, pos_count):
    n_blk, blk, width = blocks.shape
    rows = mine[0][0].shape[2]
    step_rows = min(STEP_ROWS, rows)
    at = row // step_rows
    n_doc = docs.shape[0]
    first = carry is None
    full = lambda a: pl.BlockSpec(a, lambda i: (0, 0), pipeline_mode=pl.Buffered(1))
    rowed = lambda n: pl.BlockSpec((n_blk, step_rows, n), lambda i: (0, at + i, 0))
    in_specs = [SMEM, SMEM, SMEM, SMEM]
    args = [pos, table, inv, near]
    for group in mine:
        in_specs += [slot_spec(a, step_rows, 0) for a in group]
        args += list(group)
    for group in sums:
        in_specs += [pl.BlockSpec((n_blk, step_rows, width // 2), lambda i: (0, i, 0))] * 2
        args += list(group)
    in_specs += [rowed(width), full(labels.shape), full(weight.shape), full(docs.shape)]
    args += [blocks, labels, weight, docs]
    aliases = {}
    if not first:
        hid, gd, gw = carry
        in_specs += [full(gd.shape), full(gw.shape), pl.BlockSpec(memory_space=pl.ANY)]
        aliases = {len(args) + 2: 0}
        args += [gd, gw, hid]
    return pl.pallas_call(
        functools.partial(head_kernel, first, row, blk, labels_total, pos_count),
        grid=(rows // step_rows,),
        in_specs=in_specs,
        out_specs=[rowed(width),
                   pl.BlockSpec((n_doc, width), lambda i: (0, 0)),
                   pl.BlockSpec((width, width), lambda i: (0, 0))],
        out_shape=[jax.ShapeDtypeStruct(blocks.shape, BF),
                   jax.ShapeDtypeStruct((n_doc, width), F32),
                   jax.ShapeDtypeStruct((width, width), F32)],
        scratch_shapes=[pltpu.VMEM((n_blk, step_rows, width), F32),
                        pltpu.VMEM((n_blk * step_rows, width), BF),
                        pltpu.VMEM((n_blk * step_rows, n_doc), BF)],
        input_output_aliases=aliases,
        compiler_params=pltpu.CompilerParams(vmem_limit_bytes=48 << 20),
        name=f"head_{row}",
    )(*args)


def swap(x, axis):
    return lax.all_to_all(x, axis, split_axis=0, concat_axis=0, tiled=True)


def spread(x, axis, n):
    return swap(jnp.broadcast_to(x[None], (n,) + x.shape), axis)


def per_device(emb, tiles, msg_src, msg_dst, msg_count, weight, docs, doc_labels):
    n_col = lax.axis_size("col")
    n_row = lax.axis_size("row")
    label_dev, width = emb.shape
    n_peer, cap, blk, _ = tiles.shape
    blk_dev = label_dev // blk
    labels_total = float(label_dev * n_row * n_col)
    pos_count = doc_labels.shape[1]
    n_doc = docs.shape[0] * n_row
    blocks = emb.reshape(blk_dev, blk, width)
    col = lax.axis_index("col")
    y, x = col // RING, col % RING
    pos = jnp.stack([y, x]).astype(jnp.int32)
    steps = jnp.arange(n_peer, dtype=jnp.int32)
    outer, inner = steps // RING, steps % RING
    orders = (wrap(y + inner) * RING + wrap(x + outer), wrap(y + outer) * RING + wrap(x + inner))
    axes = (("x", "y"), ("y", "x"))

    n_chunk = len(CHUNK_ROWS)
    starts = [sum(CHUNK_ROWS[:k]) for k in range(n_chunk)]
    came = [[None, None] for _ in CHUNK_ROWS]
    for k, (row, rows) in enumerate(zip(starts, CHUNK_ROWS)):
        for half in range(2):
            out = messages_of(orders[half], msg_src, blocks, tiles, row, rows, half)
            came[k][half] = [out[0]] + [shift(out[j], axes[half][0], j) for j in range(1, RING)]

    table = jnp.concatenate([msg_dst, msg_count], axis=1).reshape(-1)
    table = spread(table, "col", n_col).reshape(n_col, n_col * 2 * cap)
    arrive = lax.dynamic_slice_in_dim(table, col * 2 * cap, 2 * cap, 1)
    dst = arrive[:, :cap].reshape(-1)
    cnt = arrive[:, cap:].reshape(-1).astype(F32)
    hot = dst[None, :] == jnp.arange(blk_dev, dtype=jnp.int32)[:, None]
    inv = 1.0 / (float(blk) + jnp.sum(jnp.where(hot, cnt[None, :], 0.0), axis=1))

    all_docs = spread(docs, "row", n_row).reshape(n_doc, width)
    base = (lax.axis_index("row") * n_col + col) * label_dev
    labels = doc_labels.T - base
    group = jnp.where((labels >= 0) & (labels < label_dev), labels // STEP_ROWS, -1).reshape(-1)
    near = jnp.max((group[None, :] == jnp.arange(label_dev // STEP_ROWS)[:, None]).astype(jnp.int32),
                   axis=1)

    carry = None
    for k, row in enumerate(starts):
        sums = []
        for half in range(2):
            second = axes[half][1]
            after = [came[k + 1][h][0] for h in range(2)] if k + 1 < n_chunk else []
            after = after + [all_docs] if k == 0 else after
            low, high = far_sums(half, pos, table, came[k][half], blk_dev, after)
            low, high = shift(low, second, 1), shift(high, second, -1)
            up, down = near_sums(half, pos, table, came[k][half], low, high)
            sums.append((shift(up, second, 1), shift(down, second, -1)))
        carry = head(pos, table, inv, near, came[k], sums, blocks, labels, weight, all_docs, carry,
                     row, labels_total, float(pos_count))
    hidden, gd, gw = carry

    both = jnp.concatenate([gd, gw], axis=1).astype(BF)
    share = n_doc // n_col
    part = swap(both.reshape(n_col, share, 2 * width), "col")
    part = jnp.sum(part.astype(F32), axis=0).astype(BF)
    part = spread(part, "row", n_row)
    part = jnp.sum(part.astype(F32), axis=0).astype(BF)
    whole = spread(part, "col", n_col).reshape(n_doc, 2 * width)
    mine = lax.dynamic_slice_in_dim(
        whole[:, :width], lax.axis_index("row") * docs.shape[0], docs.shape[0], 0
    )
    return (hidden.reshape(label_dev, width), mine.astype(F32), whole[:, width:].astype(F32))


def solution(mesh):
    in_specs = (
        P(("row", "col"), None),
        P(("row", "col"), None, None, None),
        P(("row", "col"), None),
        P(("row", "col"), None),
        P(("row", "col"), None),
        P(),
        P("row", None),
        P(),
    )
    out_specs = (P(("row", "col"), None), P("row", None), P())
    return jax.shard_map(
        per_device, mesh=mesh, in_specs=in_specs, out_specs=out_specs, check_vma=False
    )
```

```python
import functools

import jax
import jax.numpy as jnp
from jax import lax
from jax.experimental import pallas as pl
from jax.experimental.pallas import tpu as pltpu
from jax.sharding import PartitionSpec as P


BF = jnp.bfloat16
F32 = jnp.float32
CHUNK_ROWS = (192, 64)
STEP_ROWS = 32
RING = 4


def wrap(i):
    return lax.rem(i + RING, RING)


def shift_pairs(axis, by):
    pairs = []
    for y in range(RING):
        for x in range(RING):
            ty, tx = ((y + by) % RING, x) if axis == "y" else (y, (x + by) % RING)
            pairs.append((y * RING + x, ty * RING + tx))
    return pairs


def shift(v, axis, by):
    return lax.ppermute(v, "col", shift_pairs(axis, by))


def message_kernel(order_ref, src_ref, emb_ref, *refs):
    d = pl.program_id(0)
    for j in range(RING):
        tile_ref, out_ref = refs[j], refs[j - RING]
        p = order_ref[j * RING + d]
        for q in range(tile_ref.shape[1]):
            out_ref[0, q] = jnp.dot(
                tile_ref[0, q], emb_ref[src_ref[p, q]], preferred_element_type=F32
            ).astype(BF)


def messages_of(order, src, blocks, tiles, row, rows, half, after):
    _, cap, blk, _ = tiles.shape
    n_blk, _, width = blocks.shape
    at = row // rows
    part = width // 2
    shape = (RING, cap, rows, part)
    return pl.pallas_call(
        message_kernel,
        grid_spec=pltpu.PrefetchScalarGridSpec(
            num_scalar_prefetch=2,
            grid=(RING,),
            in_specs=[
                pl.BlockSpec((n_blk, blk, part), lambda i, o, s: (0, 0, half),
                             pipeline_mode=pl.Buffered(1)),
            ] + [
                pl.BlockSpec((1, cap, rows, blk),
                             lambda i, o, s, j=j: (o[j * RING + i], 0, at, 0))
                for j in range(RING)
            ] + [pl.BlockSpec(memory_space=pl.ANY)] * len(after),
            out_specs=[pl.BlockSpec((1,) + shape[1:], lambda i, o, s: (i, 0, 0, 0))] * RING,
        ),
        out_shape=[jax.ShapeDtypeStruct(shape, BF)] * RING,
    )(order, src, blocks, *[tiles] * RING, *after)


def add_slots(acc_ref, table_ref, y, x, half, ahead, parts, columns):
    n_blk = acc_ref.shape[0]
    cap = parts[0].shape[1]
    for came, ref in enumerate(parts):
        if half == 0:
            s = y * RING + wrap(x - came)
            p = wrap(y + ahead) * RING + x
        else:
            s = wrap(y - came) * RING + x
            p = y * RING + wrap(x + ahead)

        def add(q, carry):
            dst = table_ref[s, p * 2 * cap + q]
            cnt = table_ref[s, p * 2 * cap + cap + q].astype(F32)

            @pl.when(dst < n_blk)
            def _():
                acc_ref[dst, :, columns] = (
                    acc_ref[dst, :, columns] + cnt * ref[0, q].astype(F32)
                )

            return carry

        lax.fori_loop(0, cap, add, 0)


def far_kernel(half, pos_ref, table_ref, *refs):
    parts, (low_ref, high_ref, acc_ref) = refs[:RING], refs[-3:]
    acc_ref[...] = jnp.zeros_like(acc_ref)
    add_slots(acc_ref, table_ref, pos_ref[0], pos_ref[1], half, 2, parts, slice(None))
    n = low_ref.shape[0]
    low_ref[...] = acc_ref[:n].astype(BF)
    high_ref[...] = acc_ref[n:].astype(BF)


def near_kernel(half, pos_ref, table_ref, *refs):
    ones, threes = refs[:RING], refs[RING:2 * RING]
    low_in, high_in, up_ref, down_ref, acc_ref = refs[2 * RING:]
    n = low_in.shape[0]
    acc_ref[:n] = low_in[...].astype(F32)
    acc_ref[n:] = jnp.zeros_like(acc_ref[n:])
    add_slots(acc_ref, table_ref, pos_ref[0], pos_ref[1], half, 1, ones, slice(None))
    up_ref[...] = acc_ref[...].astype(BF)
    acc_ref[:n] = jnp.zeros_like(acc_ref[:n])
    acc_ref[n:] = high_in[...].astype(F32)
    add_slots(acc_ref, table_ref, pos_ref[0], pos_ref[1], half, 3, threes, slice(None))
    down_ref[...] = acc_ref[...].astype(BF)


SMEM = pl.BlockSpec(memory_space=pltpu.SMEM)


def slot_spec(part, step_rows, ahead):
    return pl.BlockSpec((1, part.shape[1], step_rows, part.shape[3]),
                        lambda i: (ahead, 0, i, 0))


def far_sums(half, pos, table, parts, n_blk, after):
    _, _, rows, cols = parts[0].shape
    step_rows = min(STEP_ROWS, rows)
    n = n_blk // 2
    return pl.pallas_call(
        functools.partial(far_kernel, half),
        grid=(rows // step_rows,),
        in_specs=[SMEM, SMEM] + [slot_spec(a, step_rows, 2) for a in parts]
        + [pl.BlockSpec(memory_space=pl.ANY)] * len(after),
        out_specs=[pl.BlockSpec((n, step_rows, cols), lambda i: (0, i, 0))] * 2,
        out_shape=[jax.ShapeDtypeStruct((n, rows, cols), BF)] * 2,
        scratch_shapes=[pltpu.VMEM((n_blk, step_rows, cols), F32)],
    )(pos, table, *parts, *after)


def near_sums(half, pos, table, parts, low, high):
    _, _, rows, cols = parts[0].shape
    step_rows = min(STEP_ROWS, rows)
    n = low.shape[0]
    rowed = lambda k: pl.BlockSpec((k, step_rows, cols), lambda i: (0, i, 0))
    return pl.pallas_call(
        functools.partial(near_kernel, half),
        grid=(rows // step_rows,),
        in_specs=[SMEM, SMEM] + [slot_spec(a, step_rows, 1) for a in parts]
        + [slot_spec(a, step_rows, 3) for a in parts] + [rowed(n), rowed(n)],
        out_specs=[rowed(2 * n)] * 2,
        out_shape=[jax.ShapeDtypeStruct((2 * n, rows, cols), BF)] * 2,
        scratch_shapes=[pltpu.VMEM((2 * n, step_rows, cols), F32)],
    )(pos, table, *parts, *parts, low, high)


def head_kernel(first, row, blk, labels_total, pos_count,
                pos_ref, table_ref, inv_ref, near_ref, *refs):
    mine = (refs[:RING], refs[RING:2 * RING])
    refs = refs[2 * RING:]
    sums = (refs[:2], refs[2:4])
    emb_ref, labels_ref, w_ref, docs_ref = refs[4:8]
    rest = refs[8:]
    if first:
        hid_ref, gd_ref, gw_ref, acc_ref, agg_ref, ds_ref = rest
    else:
        gd_in, gw_in, _, hid_ref, gd_ref, gw_ref, acc_ref, agg_ref, ds_ref = rest
    step = pl.program_id(0)

    @pl.when(step == 0)
    def _():
        if first:
            gd_ref[...] = jnp.zeros_like(gd_ref)
            gw_ref[...] = jnp.zeros_like(gw_ref)
        else:
            gd_ref[...] = gd_in[...]
            gw_ref[...] = gw_in[...]

    n_blk, rows, width = emb_ref.shape
    part = width // 2
    for half in range(2):
        columns = slice(half * part, (half + 1) * part)
        up, down = sums[half]
        for b in range(n_blk):
            acc_ref[b, :, columns] = (
                float(blk) * emb_ref[b, :, columns].astype(F32)
                + up[b].astype(F32) + down[b].astype(F32)
            )
        add_slots(acc_ref, table_ref, pos_ref[0], pos_ref[1], half, 0, mine[half], columns)
    for b in range(n_blk):
        agg_ref[b * rows:(b + 1) * rows, :] = (acc_ref[b] * inv_ref[b]).astype(BF)
    agg = agg_ref[...]
    pre = jnp.dot(agg, w_ref[...], preferred_element_type=F32)
    sig = 1.0 / (1.0 + jnp.exp(-pre))
    hid = (pre * sig).astype(BF)
    for b in range(n_blk):
        hid_ref[b] = hid[b * rows:(b + 1) * rows, :]
    scores = lax.dot_general(hid, docs_ref[...], (((1,), (1,)), ((), ())),
                             preferred_element_type=F32)
    prob = 1.0 / (1.0 + jnp.exp(-scores))
    for b in range(n_blk):
        one = prob[b * rows:(b + 1) * rows, :]
        ds_ref[b * rows:(b + 1) * rows, :] = (one * (1.0 / labels_total)).astype(BF)

        @pl.when(near_ref[(b * blk + row) // rows + step] > 0)
        def _():
            ids = b * blk + row + step * rows + lax.broadcasted_iota(jnp.int32, one.shape, 0)
            hit = labels_ref[0:1, :] == ids
            for j in range(1, labels_ref.shape[0]):
                hit = hit | (labels_ref[j:j + 1, :] == ids)
            ds_ref[b * rows:(b + 1) * rows, :] = jnp.where(
                hit, (one - 1.0) * (1.0 / pos_count), one * (1.0 / labels_total)
            ).astype(BF)
    ds = ds_ref[...]
    gd_ref[...] += lax.dot_general(ds, hid, (((0,), (0,)), ((), ())),
                                   preferred_element_type=F32)
    dhid = jnp.dot(ds, docs_ref[...], preferred_element_type=F32)
    dpre = (dhid * sig * (1.0 + pre * (1.0 - sig))).astype(BF)
    gw_ref[...] += lax.dot_general(agg, dpre, (((0,), (0,)), ((), ())),
                                   preferred_element_type=F32)


def head(pos, table, inv, near, mine, sums, blocks, labels, weight, docs, carry, row,
         labels_total, pos_count):
    n_blk, blk, width = blocks.shape
    rows = mine[0][0].shape[2]
    step_rows = min(STEP_ROWS, rows)
    at = row // step_rows
    n_doc = docs.shape[0]
    first = carry is None
    full = lambda a: pl.BlockSpec(a, lambda i: (0, 0), pipeline_mode=pl.Buffered(1))
    rowed = lambda n: pl.BlockSpec((n_blk, step_rows, n), lambda i: (0, at + i, 0))
    in_specs = [SMEM, SMEM, SMEM, SMEM]
    args = [pos, table, inv, near]
    for group in mine:
        in_specs += [slot_spec(a, step_rows, 0) for a in group]
        args += list(group)
    for group in sums:
        in_specs += [pl.BlockSpec((n_blk, step_rows, width // 2), lambda i: (0, i, 0))] * 2
        args += list(group)
    in_specs += [rowed(width), full(labels.shape), full(weight.shape), full(docs.shape)]
    args += [blocks, labels, weight, docs]
    aliases = {}
    if not first:
        hid, gd, gw = carry
        in_specs += [full(gd.shape), full(gw.shape), pl.BlockSpec(memory_space=pl.ANY)]
        aliases = {len(args) + 2: 0}
        args += [gd, gw, hid]
    return pl.pallas_call(
        functools.partial(head_kernel, first, row, blk, labels_total, pos_count),
        grid=(rows // step_rows,),
        in_specs=in_specs,
        out_specs=[rowed(width),
                   pl.BlockSpec((n_doc, width), lambda i: (0, 0)),
                   pl.BlockSpec((width, width), lambda i: (0, 0))],
        out_shape=[jax.ShapeDtypeStruct(blocks.shape, BF),
                   jax.ShapeDtypeStruct((n_doc, width), F32),
                   jax.ShapeDtypeStruct((width, width), F32)],
        scratch_shapes=[pltpu.VMEM((n_blk, step_rows, width), F32),
                        pltpu.VMEM((n_blk * step_rows, width), BF),
                        pltpu.VMEM((n_blk * step_rows, n_doc), BF)],
        input_output_aliases=aliases,
        compiler_params=pltpu.CompilerParams(vmem_limit_bytes=48 << 20),
    )(*args)


def swap(x, axis):
    return lax.all_to_all(x, axis, split_axis=0, concat_axis=0, tiled=True)


def spread(x, axis, n):
    return swap(jnp.broadcast_to(x[None], (n,) + x.shape), axis)


def per_device(emb, tiles, msg_src, msg_dst, msg_count, weight, docs, doc_labels):
    n_col = lax.axis_size("col")
    n_row = lax.axis_size("row")
    label_dev, width = emb.shape
    n_peer, cap, blk, _ = tiles.shape
    blk_dev = label_dev // blk
    labels_total = float(label_dev * n_row * n_col)
    pos_count = doc_labels.shape[1]
    n_doc = docs.shape[0] * n_row
    blocks = emb.reshape(blk_dev, blk, width)
    col = lax.axis_index("col")
    y, x = col // RING, col % RING
    pos = jnp.stack([y, x]).astype(jnp.int32)
    steps = jnp.arange(n_peer, dtype=jnp.int32)
    outer, inner = steps // RING, steps % RING
    orders = (wrap(y + inner) * RING + wrap(x + outer), wrap(y + outer) * RING + wrap(x + inner))
    axes = (("x", "y"), ("y", "x"))

    table = jnp.concatenate([msg_dst, msg_count], axis=1).reshape(-1)
    table = spread(table, "col", n_col).reshape(n_col, n_col * 2 * cap)
    share = docs.shape[0] // n_col
    regroup = lambda a: a.reshape((n_row, n_col, share) + a.shape[1:]).swapaxes(0, 1).reshape(a.shape)
    gathered = spread(docs, "row", n_row).reshape(n_doc, width)
    all_docs = regroup(gathered)
    base = (lax.axis_index("row") * n_col + col) * label_dev
    labels = regroup(doc_labels).T - base

    n_chunk = len(CHUNK_ROWS)
    starts = [sum(CHUNK_ROWS[:k]) for k in range(n_chunk)]
    came = [[None, None] for _ in CHUNK_ROWS]
    lows = [[None, None] for _ in CHUNK_ROWS]
    ends = [[None, None] for _ in CHUNK_ROWS]

    def send(k):
        for half in range(2):
            after = {(0, 1): [table], (1, 1): [gathered]}.get((k, half), [])
            after = after + lows[k - 2] if k >= 2 else after
            out = messages_of(orders[half], msg_src, blocks, tiles,
                        starts[k], CHUNK_ROWS[k], half, after)
            came[k][half] = [out[0]] + [shift(out[j], axes[half][0], j) for j in range(1, RING)]

    def combine(k):
        for half in range(2):
            second = axes[half][1]
            after = [came[k + 1][h][0] for h in range(2)] if k + 1 < n_chunk else []
            low, high = far_sums(half, pos, table, came[k][half],
                              blk_dev, after)
            lows[k][half] = low
            ends[k][half] = (shift(low, second, 1),
                             shift(high, second, -1))

    send(0)
    for k in range(n_chunk):
        if k + 1 < n_chunk:
            send(k + 1)
        combine(k)

    arrive = lax.dynamic_slice_in_dim(table, col * 2 * cap, 2 * cap, 1)
    dst = arrive[:, :cap].reshape(-1)
    cnt = arrive[:, cap:].reshape(-1).astype(F32)
    hot = dst[None, :] == jnp.arange(blk_dev, dtype=jnp.int32)[:, None]
    inv = 1.0 / (float(blk) + jnp.sum(jnp.where(hot, cnt[None, :], 0.0), axis=1))
    group = jnp.where((labels >= 0) & (labels < label_dev), labels // STEP_ROWS, -1).reshape(-1)
    near = jnp.max((group[None, :] == jnp.arange(label_dev // STEP_ROWS)[:, None]).astype(jnp.int32),
                   axis=1)

    carry = None
    for k, row in enumerate(starts):
        sums = []
        for half in range(2):
            second = axes[half][1]
            up, down = near_sums(half, pos, table, came[k][half],
                             *ends[k][half])
            sums.append((shift(up, second, 1),
                         shift(down, second, -1)))
        carry = head(pos, table, inv, near, came[k], sums, blocks, labels, weight, all_docs, carry,
                     row, labels_total, float(pos_count))
    hidden, gd, gw = carry

    part_of = n_doc // n_col
    lane = width // share
    both = jnp.concatenate([gd, gw], axis=1).astype(BF)
    part = swap(both.reshape(n_col, part_of, 2 * width), "col")
    part = jnp.sum(part.astype(F32), axis=0).astype(BF)
    own = part[:, :width].reshape(n_row, share * share, lane)
    own = jnp.pad(own, ((0, 0), (0, part_of - share * share), (0, 0)))
    out = jnp.broadcast_to(part[None, :, width:], (n_row, part_of, width))
    part = swap(jnp.concatenate([out, own], axis=2), "row")
    part = jnp.sum(part.astype(F32), axis=0).astype(BF)
    whole = spread(part, "col", n_col)
    grad_weight = whole[:, :, :width].reshape(n_doc, width)
    grad_docs = whole[:, :share * share, width:].reshape(docs.shape)
    return hidden.reshape(label_dev, width), grad_docs.astype(F32), grad_weight.astype(F32)


def solution(mesh):
    in_specs = (
        P(("row", "col"), None),
        P(("row", "col"), None, None, None),
        P(("row", "col"), None),
        P(("row", "col"), None),
        P(("row", "col"), None),
        P(),
        P("row", None),
        P(),
    )
    out_specs = (P(("row", "col"), None), P("row", None), P())

    return jax.shard_map(
        per_device, mesh=mesh, in_specs=in_specs, out_specs=out_specs, check_vma=False
    )
```

```python
import functools

import jax
import jax.numpy as jnp
from jax import lax
from jax.experimental import pallas as pl
from jax.experimental.pallas import tpu as pltpu
from jax.sharding import PartitionSpec as P


BF = jnp.bfloat16
F32 = jnp.float32
CHUNK_ROWS = (128, 128)
SUM_ROWS = 128
STEP_ROWS = 64
RING = 4


def wrap(i):
    return lax.rem(i + RING, RING)


def shift_pairs(axis, by):
    pairs = []
    for y in range(RING):
        for x in range(RING):
            ty, tx = ((y + by) % RING, x) if axis == "y" else (y, (x + by) % RING)
            pairs.append((y * RING + x, ty * RING + tx))
    return pairs


def shift(v, axis, by):
    return lax.ppermute(v, "col", shift_pairs(axis, by))


def message_kernel(order_ref, src_ref, emb_ref, *refs):
    d = pl.program_id(0)
    for j in range(RING):
        tile_ref, out_ref = refs[j], refs[j - RING]
        p = order_ref[j * RING + d]
        for q in range(tile_ref.shape[1]):
            out_ref[0, q] = jnp.dot(
                tile_ref[0, q], emb_ref[src_ref[p, q]], preferred_element_type=F32
            ).astype(BF)


def messages_of(order, src, blocks, tiles, row, rows, half, after):
    _, cap, blk, _ = tiles.shape
    n_blk, _, width = blocks.shape
    at = row // rows
    part = width // 2
    shape = (RING, cap, rows, part)
    return pl.pallas_call(
        message_kernel,
        grid_spec=pltpu.PrefetchScalarGridSpec(
            num_scalar_prefetch=2,
            grid=(RING,),
            in_specs=[
                pl.BlockSpec((n_blk, blk, part), lambda i, o, s: (0, 0, half),
                             pipeline_mode=pl.Buffered(1)),
            ] + [
                pl.BlockSpec((1, cap, rows, blk),
                             lambda i, o, s, j=j: (o[j * RING + i], 0, at, 0))
                for j in range(RING)
            ] + [pl.BlockSpec(memory_space=pl.ANY)] * len(after),
            out_specs=[pl.BlockSpec((1,) + shape[1:], lambda i, o, s: (i, 0, 0, 0))] * RING,
        ),
        out_shape=[jax.ShapeDtypeStruct(shape, BF)] * RING,
    )(order, src, blocks, *[tiles] * RING, *after)


def add_slots(acc_ref, table_ref, y, x, half, ahead, parts, columns):
    n_blk = acc_ref.shape[0]
    cap = parts[0].shape[1]
    for came, ref in enumerate(parts):
        if half == 0:
            s = y * RING + wrap(x - came)
            p = wrap(y + ahead) * RING + x
        else:
            s = wrap(y - came) * RING + x
            p = y * RING + wrap(x + ahead)

        def add(q, carry):
            dst = table_ref[s, p * 2 * cap + q]
            cnt = table_ref[s, p * 2 * cap + cap + q].astype(F32)

            @pl.when(dst < n_blk)
            def _():
                acc_ref[dst, :, columns] = (
                    acc_ref[dst, :, columns] + cnt * ref[0, q].astype(F32)
                )

            return carry

        lax.fori_loop(0, cap, add, 0)


def far_kernel(half, pos_ref, table_ref, *refs):
    parts, (low_ref, high_ref, acc_ref) = refs[:RING], refs[-3:]
    acc_ref[...] = jnp.zeros_like(acc_ref)
    add_slots(acc_ref, table_ref, pos_ref[0], pos_ref[1], half, 2, parts, slice(None))
    n = low_ref.shape[0]
    low_ref[...] = acc_ref[:n].astype(BF)
    high_ref[...] = acc_ref[n:].astype(BF)


def near_kernel(half, pos_ref, table_ref, *refs):
    ones, threes = refs[:RING], refs[RING:2 * RING]
    low_in, high_in, up_ref, down_ref, acc_ref = refs[2 * RING:]
    n = low_in.shape[0]
    acc_ref[:n] = low_in[...].astype(F32)
    acc_ref[n:] = jnp.zeros_like(acc_ref[n:])
    add_slots(acc_ref, table_ref, pos_ref[0], pos_ref[1], half, 1, ones, slice(None))
    up_ref[...] = acc_ref[...].astype(BF)
    acc_ref[:n] = jnp.zeros_like(acc_ref[:n])
    acc_ref[n:] = high_in[...].astype(F32)
    add_slots(acc_ref, table_ref, pos_ref[0], pos_ref[1], half, 3, threes, slice(None))
    down_ref[...] = acc_ref[...].astype(BF)


SMEM = pl.BlockSpec(memory_space=pltpu.SMEM)


def slot_spec(part, step_rows, ahead):
    return pl.BlockSpec((1, part.shape[1], step_rows, part.shape[3]),
                        lambda i: (ahead, 0, i, 0))


def far_sums(half, pos, table, parts, n_blk, after):
    _, _, rows, cols = parts[0].shape
    step_rows = min(SUM_ROWS, rows)
    n = n_blk // 2
    return pl.pallas_call(
        functools.partial(far_kernel, half),
        grid=(rows // step_rows,),
        in_specs=[SMEM, SMEM] + [slot_spec(a, step_rows, 2) for a in parts]
        + [pl.BlockSpec(memory_space=pl.ANY)] * len(after),
        out_specs=[pl.BlockSpec((n, step_rows, cols), lambda i: (0, i, 0))] * 2,
        out_shape=[jax.ShapeDtypeStruct((n, rows, cols), BF)] * 2,
        scratch_shapes=[pltpu.VMEM((n_blk, step_rows, cols), F32)],
    )(pos, table, *parts, *after)


def near_sums(half, pos, table, parts, low, high):
    _, _, rows, cols = parts[0].shape
    step_rows = min(SUM_ROWS, rows)
    n = low.shape[0]
    rowed = lambda k: pl.BlockSpec((k, step_rows, cols), lambda i: (0, i, 0))
    return pl.pallas_call(
        functools.partial(near_kernel, half),
        grid=(rows // step_rows,),
        in_specs=[SMEM, SMEM] + [slot_spec(a, step_rows, 1) for a in parts]
        + [slot_spec(a, step_rows, 3) for a in parts] + [rowed(n), rowed(n)],
        out_specs=[rowed(2 * n)] * 2,
        out_shape=[jax.ShapeDtypeStruct((2 * n, rows, cols), BF)] * 2,
        scratch_shapes=[pltpu.VMEM((2 * n, step_rows, cols), F32)],
    )(pos, table, *parts, *parts, low, high)


def head_kernel(first, last, row, blk, labels_total, pos_count,
                pos_ref, table_ref, inv_ref, near_ref, *refs):
    mine = (refs[:RING], refs[RING:2 * RING])
    refs = refs[2 * RING:]
    sums = (refs[:2], refs[2:4])
    emb_ref, labels_ref, w_ref, docs_ref = refs[4:8]
    rest = refs[8:]
    if not first:
        gd_in, gw_in, _ = rest[:3]
        rest = rest[3:]
    if last:
        hid_ref, both_ref, acc_ref, agg_ref, ds_ref, gd_ref, gw_ref = rest
    else:
        hid_ref, gd_ref, gw_ref, acc_ref, agg_ref, ds_ref = rest
    step = pl.program_id(0)

    @pl.when(step == 0)
    def _():
        if first:
            gd_ref[...] = jnp.zeros_like(gd_ref)
            gw_ref[...] = jnp.zeros_like(gw_ref)
        else:
            gd_ref[...] = gd_in[...]
            gw_ref[...] = gw_in[...]

    n_blk, rows, width = emb_ref.shape
    part = width // 2
    for half in range(2):
        columns = slice(half * part, (half + 1) * part)
        up, down = sums[half]
        for b in range(n_blk):
            acc_ref[b, :, columns] = (
                float(blk) * emb_ref[b, :, columns].astype(F32)
                + up[b].astype(F32) + down[b].astype(F32)
            )
        add_slots(acc_ref, table_ref, pos_ref[0], pos_ref[1], half, 0, mine[half], columns)
    for b in range(n_blk):
        agg_ref[b * rows:(b + 1) * rows, :] = (acc_ref[b] * inv_ref[b]).astype(BF)
    agg = agg_ref[...]
    pre = jnp.dot(agg, w_ref[...], preferred_element_type=F32)
    sig = 1.0 / (1.0 + jnp.exp(-pre))
    hid = (pre * sig).astype(BF)
    for b in range(n_blk):
        hid_ref[b] = hid[b * rows:(b + 1) * rows, :]
    scores = lax.dot_general(hid, docs_ref[...], (((1,), (1,)), ((), ())),
                             preferred_element_type=F32)
    prob = 1.0 / (1.0 + jnp.exp(-scores))
    for b in range(n_blk):
        one = prob[b * rows:(b + 1) * rows, :]
        ds_ref[b * rows:(b + 1) * rows, :] = (one * (1.0 / labels_total)).astype(BF)

        @pl.when(near_ref[(b * blk + row) // rows + step] > 0)
        def _():
            ids = b * blk + row + step * rows + lax.broadcasted_iota(jnp.int32, one.shape, 0)
            hit = labels_ref[0:1, :] == ids
            for j in range(1, labels_ref.shape[0]):
                hit = hit | (labels_ref[j:j + 1, :] == ids)
            ds_ref[b * rows:(b + 1) * rows, :] = jnp.where(
                hit, (one - 1.0) * (1.0 / pos_count), one * (1.0 / labels_total)
            ).astype(BF)
    ds = ds_ref[...]
    gd_ref[...] += lax.dot_general(ds, hid, (((0,), (0,)), ((), ())),
                                   preferred_element_type=F32)
    dhid = jnp.dot(ds, docs_ref[...], preferred_element_type=F32)
    dpre = (dhid * sig * (1.0 + pre * (1.0 - sig))).astype(BF)
    gw_ref[...] += lax.dot_general(agg, dpre, (((0,), (0,)), ((), ())),
                                   preferred_element_type=F32)
    if last:
        @pl.when(step == pl.num_programs(0) - 1)
        def _():
            both_ref[:, :width] = gd_ref[...].astype(BF)
            both_ref[:, width:] = gw_ref[...].astype(BF)


def head(pos, table, inv, near, mine, sums, blocks, labels, weight, docs, carry, row,
         last, labels_total, pos_count):
    n_blk, blk, width = blocks.shape
    rows = mine[0][0].shape[2]
    step_rows = min(STEP_ROWS, rows)
    at = row // step_rows
    n_doc = docs.shape[0]
    first = carry is None
    full = lambda a: pl.BlockSpec(a, lambda i: (0, 0), pipeline_mode=pl.Buffered(1))
    rowed = lambda n: pl.BlockSpec((n_blk, step_rows, n), lambda i: (0, at + i, 0))
    in_specs = [SMEM, SMEM, SMEM, SMEM]
    args = [pos, table, inv, near]
    for group in mine:
        in_specs += [slot_spec(a, step_rows, 0) for a in group]
        args += list(group)
    for group in sums:
        in_specs += [pl.BlockSpec((n_blk, step_rows, width // 2), lambda i: (0, i, 0))] * 2
        args += list(group)
    in_specs += [rowed(width), full(labels.shape), full(weight.shape), full(docs.shape)]
    args += [blocks, labels, weight, docs]
    aliases = {}
    if not first:
        hid, gd, gw = carry
        in_specs += [full(gd.shape), full(gw.shape), pl.BlockSpec(memory_space=pl.ANY)]
        aliases = {len(args) + 2: 0}
        args += [gd, gw, hid]
    grads = [((n_doc, 2 * width), BF)] if last else [((n_doc, width), F32), ((width, width), F32)]
    return pl.pallas_call(
        functools.partial(head_kernel, first, last, row, blk, labels_total, pos_count),
        grid=(rows // step_rows,),
        in_specs=in_specs,
        out_specs=[rowed(width)] + [pl.BlockSpec(a, lambda i: (0, 0)) for a, _ in grads],
        out_shape=[jax.ShapeDtypeStruct(blocks.shape, BF)]
        + [jax.ShapeDtypeStruct(a, t) for a, t in grads],
        scratch_shapes=[pltpu.VMEM((n_blk, step_rows, width), F32),
                        pltpu.VMEM((n_blk * step_rows, width), BF),
                        pltpu.VMEM((n_blk * step_rows, n_doc), BF)]
        + ([pltpu.VMEM((n_doc, width), F32), pltpu.VMEM((width, width), F32)] if last else []),
        input_output_aliases=aliases,
        compiler_params=pltpu.CompilerParams(vmem_limit_bytes=48 << 20),
    )(*args)


def swap(x, axis):
    return lax.all_to_all(x, axis, split_axis=0, concat_axis=0, tiled=True)


def spread(x, axis, n):
    return swap(jnp.broadcast_to(x[None], (n,) + x.shape), axis)


def per_device(emb, tiles, msg_src, msg_dst, msg_count, weight, docs, doc_labels):
    n_col = lax.axis_size("col")
    n_row = lax.axis_size("row")
    label_dev, width = emb.shape
    n_peer, cap, blk, _ = tiles.shape
    blk_dev = label_dev // blk
    labels_total = float(label_dev * n_row * n_col)
    pos_count = doc_labels.shape[1]
    n_doc = docs.shape[0] * n_row
    blocks = emb.reshape(blk_dev, blk, width)
    col = lax.axis_index("col")
    y, x = col // RING, col % RING
    pos = jnp.stack([y, x]).astype(jnp.int32)
    steps = jnp.arange(n_peer, dtype=jnp.int32)
    outer, inner = steps // RING, steps % RING
    orders = (wrap(y + inner) * RING + wrap(x + outer), wrap(y + outer) * RING + wrap(x + inner))
    axes = (("x", "y"), ("y", "x"))

    table = jnp.concatenate([msg_dst, msg_count], axis=1).reshape(-1)
    table = spread(table, "col", n_col).reshape(n_col, n_col * 2 * cap)
    share = docs.shape[0] // n_col
    regroup = lambda a: a.reshape((n_row, n_col, share) + a.shape[1:]).swapaxes(0, 1).reshape(a.shape)
    gathered = spread(docs, "row", n_row).reshape(n_doc, width)
    all_docs = regroup(gathered)
    base = (lax.axis_index("row") * n_col + col) * label_dev
    labels = regroup(doc_labels).T - base

    n_chunk = len(CHUNK_ROWS)
    starts = [sum(CHUNK_ROWS[:k]) for k in range(n_chunk)]
    came = [[None, None] for _ in CHUNK_ROWS]
    lows = [[None, None] for _ in CHUNK_ROWS]
    ends = [[None, None] for _ in CHUNK_ROWS]

    def send(k):
        for half in range(2):
            after = {(0, 1): [table], (1, 1): [gathered]}.get((k, half), [])
            after = after + lows[k - 2] if k >= 2 else after
            out = messages_of(orders[half], msg_src, blocks, tiles,
                        starts[k], CHUNK_ROWS[k], half, after)
            came[k][half] = [out[0]] + [shift(out[j], axes[half][0], j) for j in range(1, RING)]

    def combine(k):
        for half in range(2):
            second = axes[half][1]
            after = [came[k + 1][h][0] for h in range(2)] if k + 1 < n_chunk else []
            low, high = far_sums(half, pos, table, came[k][half],
                              blk_dev, after)
            lows[k][half] = low
            ends[k][half] = (shift(low, second, 1),
                             shift(high, second, -1))

    send(0)
    for k in range(n_chunk):
        if k + 1 < n_chunk:
            send(k + 1)
        combine(k)

    arrive = lax.dynamic_slice_in_dim(table, col * 2 * cap, 2 * cap, 1)
    dst = arrive[:, :cap].reshape(-1)
    cnt = arrive[:, cap:].reshape(-1).astype(F32)
    hot = dst[None, :] == jnp.arange(blk_dev, dtype=jnp.int32)[:, None]
    inv = 1.0 / (float(blk) + jnp.sum(jnp.where(hot, cnt[None, :], 0.0), axis=1))
    group = jnp.where((labels >= 0) & (labels < label_dev), labels // STEP_ROWS, -1).reshape(-1)
    near = jnp.max((group[None, :] == jnp.arange(label_dev // STEP_ROWS)[:, None]).astype(jnp.int32),
                   axis=1)

    carry = None
    for k, row in enumerate(starts):
        sums = []
        for half in range(2):
            second = axes[half][1]
            up, down = near_sums(half, pos, table, came[k][half],
                             *ends[k][half])
            sums.append((shift(up, second, 1),
                         shift(down, second, -1)))
        carry = head(pos, table, inv, near, came[k], sums, blocks, labels, weight, all_docs, carry,
                     row, k == n_chunk - 1, labels_total, float(pos_count))
    hidden, both = carry

    part_of = n_doc // n_col
    lane = width // share
    part = swap(both.reshape(n_col, part_of, 2 * width), "col")
    part = jnp.sum(part.astype(F32), axis=0).astype(BF)
    own = part[:, :width].reshape(n_row, share * share, lane)
    own = jnp.pad(own, ((0, 0), (0, part_of - share * share), (0, 0)))
    out = jnp.broadcast_to(part[None, :, width:], (n_row, part_of, width))
    part = swap(jnp.concatenate([out, own], axis=2), "row")
    part = jnp.sum(part.astype(F32), axis=0).astype(BF)
    whole = spread(part, "col", n_col)
    grad_weight = whole[:, :, :width].reshape(n_doc, width)
    grad_docs = whole[:, :share * share, width:].reshape(docs.shape)
    return hidden.reshape(label_dev, width), grad_docs.astype(F32), grad_weight.astype(F32)


def solution(mesh):
    in_specs = (
        P(("row", "col"), None),
        P(("row", "col"), None, None, None),
        P(("row", "col"), None),
        P(("row", "col"), None),
        P(("row", "col"), None),
        P(),
        P("row", None),
        P(),
    )
    out_specs = (P(("row", "col"), None), P("row", None), P())

    return jax.shard_map(
        per_device, mesh=mesh, in_specs=in_specs, out_specs=out_specs, check_vma=False
    )
```

```python
import functools

import jax
import jax.numpy as jnp
from jax import lax
from jax.experimental import pallas as pl
from jax.experimental.pallas import tpu as pltpu
from jax.sharding import PartitionSpec as P


BF = jnp.bfloat16
F32 = jnp.float32
CHUNK_ROWS = (128, 128)
SUM_ROWS = 128
STEP_ROWS = 64
RING = 4


def wrap(i):
    return lax.rem(i + RING, RING)


def shift_pairs(axis, by):
    pairs = []
    for y in range(RING):
        for x in range(RING):
            ty, tx = ((y + by) % RING, x) if axis == "y" else (y, (x + by) % RING)
            pairs.append((y * RING + x, ty * RING + tx))
    return pairs


def shift(v, axis, by):
    return lax.ppermute(v, "col", shift_pairs(axis, by))


def row_shift(v, to):
    pairs = []
    for i in range(lax.axis_size("row")):
        z, core = to(i // 2, i % 2)
        pairs.append((i, z * 2 + core))
    return lax.ppermute(v, "row", pairs)


def message_kernel(order_ref, src_ref, emb_ref, *refs):
    d = pl.program_id(0)
    for j in range(RING):
        tile_ref, out_ref = refs[j], refs[j - RING]
        p = order_ref[j * RING + d]
        for q in range(tile_ref.shape[1]):
            out_ref[0, q] = jnp.dot(
                tile_ref[0, q], emb_ref[src_ref[p, q]], preferred_element_type=F32
            ).astype(BF)


def messages_of(order, src, blocks, tiles, row, rows, half, after):
    _, cap, blk, _ = tiles.shape
    n_blk, _, width = blocks.shape
    at = row // rows
    part = width // 2
    shape = (RING, cap, rows, part)
    return pl.pallas_call(
        message_kernel,
        grid_spec=pltpu.PrefetchScalarGridSpec(
            num_scalar_prefetch=2,
            grid=(RING,),
            in_specs=[
                pl.BlockSpec((n_blk, blk, part), lambda i, o, s: (0, 0, half),
                             pipeline_mode=pl.Buffered(1)),
            ] + [
                pl.BlockSpec((1, cap, rows, blk),
                             lambda i, o, s, j=j: (o[j * RING + i], 0, at, 0))
                for j in range(RING)
            ] + [pl.BlockSpec(memory_space=pl.ANY)] * len(after),
            out_specs=[pl.BlockSpec((1,) + shape[1:], lambda i, o, s: (i, 0, 0, 0))] * RING,
        ),
        out_shape=[jax.ShapeDtypeStruct(shape, BF)] * RING,
    )(order, src, blocks, *[tiles] * RING, *after)


def add_slots(acc_ref, table_ref, y, x, half, ahead, parts, columns):
    n_blk = acc_ref.shape[0]
    cap = parts[0].shape[1]
    for came, ref in enumerate(parts):
        if half == 0:
            s = y * RING + wrap(x - came)
            p = wrap(y + ahead) * RING + x
        else:
            s = wrap(y - came) * RING + x
            p = y * RING + wrap(x + ahead)

        def add(q, carry):
            dst = table_ref[s, p * 2 * cap + q]
            cnt = table_ref[s, p * 2 * cap + cap + q].astype(F32)

            @pl.when(dst < n_blk)
            def _():
                acc_ref[dst, :, columns] = (
                    acc_ref[dst, :, columns] + cnt * ref[0, q].astype(F32)
                )

            return carry

        lax.fori_loop(0, cap, add, 0)


def far_kernel(half, pos_ref, table_ref, *refs):
    parts, (low_ref, high_ref, acc_ref) = refs[:RING], refs[-3:]
    acc_ref[...] = jnp.zeros_like(acc_ref)
    add_slots(acc_ref, table_ref, pos_ref[0], pos_ref[1], half, 2, parts, slice(None))
    n = low_ref.shape[0]
    low_ref[...] = acc_ref[:n].astype(BF)
    high_ref[...] = acc_ref[n:].astype(BF)


def near_kernel(half, pos_ref, table_ref, *refs):
    ones, threes = refs[:RING], refs[RING:2 * RING]
    low_in, high_in, up_ref, down_ref, acc_ref = refs[2 * RING:]
    n = low_in.shape[0]
    acc_ref[:n] = low_in[...].astype(F32)
    acc_ref[n:] = jnp.zeros_like(acc_ref[n:])
    add_slots(acc_ref, table_ref, pos_ref[0], pos_ref[1], half, 1, ones, slice(None))
    up_ref[...] = acc_ref[...].astype(BF)
    acc_ref[:n] = jnp.zeros_like(acc_ref[:n])
    acc_ref[n:] = high_in[...].astype(F32)
    add_slots(acc_ref, table_ref, pos_ref[0], pos_ref[1], half, 3, threes, slice(None))
    down_ref[...] = acc_ref[...].astype(BF)


SMEM = pl.BlockSpec(memory_space=pltpu.SMEM)


def slot_spec(part, step_rows, ahead):
    return pl.BlockSpec((1, part.shape[1], step_rows, part.shape[3]),
                        lambda i: (ahead, 0, i, 0))


def far_sums(half, pos, table, parts, n_blk, after):
    _, _, rows, cols = parts[0].shape
    step_rows = min(SUM_ROWS, rows)
    n = n_blk // 2
    return pl.pallas_call(
        functools.partial(far_kernel, half),
        grid=(rows // step_rows,),
        in_specs=[SMEM, SMEM] + [slot_spec(a, step_rows, 2) for a in parts]
        + [pl.BlockSpec(memory_space=pl.ANY)] * len(after),
        out_specs=[pl.BlockSpec((n, step_rows, cols), lambda i: (0, i, 0))] * 2,
        out_shape=[jax.ShapeDtypeStruct((n, rows, cols), BF)] * 2,
        scratch_shapes=[pltpu.VMEM((n_blk, step_rows, cols), F32)],
    )(pos, table, *parts, *after)


def near_sums(half, pos, table, parts, low, high):
    _, _, rows, cols = parts[0].shape
    step_rows = min(SUM_ROWS, rows)
    n = low.shape[0]
    rowed = lambda k: pl.BlockSpec((k, step_rows, cols), lambda i: (0, i, 0))
    return pl.pallas_call(
        functools.partial(near_kernel, half),
        grid=(rows // step_rows,),
        in_specs=[SMEM, SMEM] + [slot_spec(a, step_rows, 1) for a in parts]
        + [slot_spec(a, step_rows, 3) for a in parts] + [rowed(n), rowed(n)],
        out_specs=[rowed(2 * n)] * 2,
        out_shape=[jax.ShapeDtypeStruct((2 * n, rows, cols), BF)] * 2,
        scratch_shapes=[pltpu.VMEM((2 * n, step_rows, cols), F32)],
    )(pos, table, *parts, *parts, low, high)


def head_kernel(first, last, row, blk, labels_total, pos_count,
                pos_ref, table_ref, inv_ref, near_ref, *refs):
    mine = (refs[:RING], refs[RING:2 * RING])
    refs = refs[2 * RING:]
    sums = (refs[:2], refs[2:4])
    emb_ref, labels_ref, w_ref, docs_ref = refs[4:8]
    rest = refs[8:]
    if not first:
        gd_in, gw_in, _ = rest[:3]
        rest = rest[3:]
    if last:
        hid_ref, both_ref, acc_ref, agg_ref, ds_ref, gd_ref, gw_ref = rest
    else:
        hid_ref, gd_ref, gw_ref, acc_ref, agg_ref, ds_ref = rest
    step = pl.program_id(0)

    @pl.when(step == 0)
    def _():
        if first:
            gd_ref[...] = jnp.zeros_like(gd_ref)
            gw_ref[...] = jnp.zeros_like(gw_ref)
        else:
            gd_ref[...] = gd_in[...]
            gw_ref[...] = gw_in[...]

    n_blk, rows, width = emb_ref.shape
    part = width // 2
    for half in range(2):
        columns = slice(half * part, (half + 1) * part)
        up, down = sums[half]
        for b in range(n_blk):
            acc_ref[b, :, columns] = (
                float(blk) * emb_ref[b, :, columns].astype(F32)
                + up[b].astype(F32) + down[b].astype(F32)
            )
        add_slots(acc_ref, table_ref, pos_ref[0], pos_ref[1], half, 0, mine[half], columns)
    for b in range(n_blk):
        agg_ref[b * rows:(b + 1) * rows, :] = (acc_ref[b] * inv_ref[b]).astype(BF)
    agg = agg_ref[...]
    pre = jnp.dot(agg, w_ref[...], preferred_element_type=F32)
    sig = 1.0 / (1.0 + jnp.exp(-pre))
    hid = (pre * sig).astype(BF)
    for b in range(n_blk):
        hid_ref[b] = hid[b * rows:(b + 1) * rows, :]
    scores = lax.dot_general(hid, docs_ref[...], (((1,), (1,)), ((), ())),
                             preferred_element_type=F32)
    prob = 1.0 / (1.0 + jnp.exp(-scores))
    for b in range(n_blk):
        one = prob[b * rows:(b + 1) * rows, :]
        ds_ref[b * rows:(b + 1) * rows, :] = (one * (1.0 / labels_total)).astype(BF)

        @pl.when(near_ref[(b * blk + row) // rows + step] > 0)
        def _():
            ids = b * blk + row + step * rows + lax.broadcasted_iota(jnp.int32, one.shape, 0)
            hit = labels_ref[0:1, :] == ids
            for j in range(1, labels_ref.shape[0]):
                hit = hit | (labels_ref[j:j + 1, :] == ids)
            ds_ref[b * rows:(b + 1) * rows, :] = jnp.where(
                hit, (one - 1.0) * (1.0 / pos_count), one * (1.0 / labels_total)
            ).astype(BF)
    ds = ds_ref[...]
    gd_ref[...] += lax.dot_general(ds, hid, (((0,), (0,)), ((), ())),
                                   preferred_element_type=F32)
    dhid = jnp.dot(ds, docs_ref[...], preferred_element_type=F32)
    dpre = (dhid * sig * (1.0 + pre * (1.0 - sig))).astype(BF)
    gw_ref[...] += lax.dot_general(agg, dpre, (((0,), (0,)), ((), ())),
                                   preferred_element_type=F32)
    if last:
        @pl.when(step == pl.num_programs(0) - 1)
        def _():
            both_ref[:, :width] = gd_ref[...].astype(BF)
            both_ref[:, width:] = gw_ref[...].astype(BF)


def head(pos, table, inv, near, mine, sums, blocks, labels, weight, docs, carry, row,
         last, labels_total, pos_count):
    n_blk, blk, width = blocks.shape
    rows = mine[0][0].shape[2]
    step_rows = min(STEP_ROWS, rows)
    at = row // step_rows
    n_doc = docs.shape[0]
    first = carry is None
    full = lambda a: pl.BlockSpec(a, lambda i: (0, 0), pipeline_mode=pl.Buffered(1))
    rowed = lambda n: pl.BlockSpec((n_blk, step_rows, n), lambda i: (0, at + i, 0))
    in_specs = [SMEM, SMEM, SMEM, SMEM]
    args = [pos, table, inv, near]
    for group in mine:
        in_specs += [slot_spec(a, step_rows, 0) for a in group]
        args += list(group)
    for group in sums:
        in_specs += [pl.BlockSpec((n_blk, step_rows, width // 2), lambda i: (0, i, 0))] * 2
        args += list(group)
    in_specs += [rowed(width), full(labels.shape), full(weight.shape), full(docs.shape)]
    args += [blocks, labels, weight, docs]
    aliases = {}
    if not first:
        hid, gd, gw = carry
        in_specs += [full(gd.shape), full(gw.shape), pl.BlockSpec(memory_space=pl.ANY)]
        aliases = {len(args) + 2: 0}
        args += [gd, gw, hid]
    grads = [((n_doc, 2 * width), BF)] if last else [((n_doc, width), F32), ((width, width), F32)]
    return pl.pallas_call(
        functools.partial(head_kernel, first, last, row, blk, labels_total, pos_count),
        grid=(rows // step_rows,),
        in_specs=in_specs,
        out_specs=[rowed(width)] + [pl.BlockSpec(a, lambda i: (0, 0)) for a, _ in grads],
        out_shape=[jax.ShapeDtypeStruct(blocks.shape, BF)]
        + [jax.ShapeDtypeStruct(a, t) for a, t in grads],
        scratch_shapes=[pltpu.VMEM((n_blk, step_rows, width), F32),
                        pltpu.VMEM((n_blk * step_rows, width), BF),
                        pltpu.VMEM((n_blk * step_rows, n_doc), BF)]
        + ([pltpu.VMEM((n_doc, width), F32), pltpu.VMEM((width, width), F32)] if last else []),
        input_output_aliases=aliases,
        compiler_params=pltpu.CompilerParams(vmem_limit_bytes=48 << 20),
    )(*args)


def swap(x, axis):
    return lax.all_to_all(x, axis, split_axis=0, concat_axis=0, tiled=True)


def spread(x, axis, n):
    return swap(jnp.broadcast_to(x[None], (n,) + x.shape), axis)


def per_device(emb, tiles, msg_src, msg_dst, msg_count, weight, docs, doc_labels):
    n_col = lax.axis_size("col")
    n_row = lax.axis_size("row")
    label_dev, width = emb.shape
    n_peer, cap, blk, _ = tiles.shape
    blk_dev = label_dev // blk
    labels_total = float(label_dev * n_row * n_col)
    pos_count = doc_labels.shape[1]
    n_doc = docs.shape[0] * n_row
    blocks = emb.reshape(blk_dev, blk, width)
    col = lax.axis_index("col")
    y, x = col // RING, col % RING
    pos = jnp.stack([y, x]).astype(jnp.int32)
    steps = jnp.arange(n_peer, dtype=jnp.int32)
    outer, inner = steps // RING, steps % RING
    orders = (wrap(y + inner) * RING + wrap(x + outer), wrap(y + outer) * RING + wrap(x + inner))
    axes = (("x", "y"), ("y", "x"))

    table = jnp.concatenate([msg_dst, msg_count], axis=1).reshape(-1)
    table = spread(table, "col", n_col).reshape(n_col, n_col * 2 * cap)
    share = docs.shape[0] // n_col
    regroup = lambda a: a.reshape((n_row, n_col, share) + a.shape[1:]).swapaxes(0, 1).reshape(a.shape)
    gathered = spread(docs, "row", n_row).reshape(n_doc, width)
    all_docs = regroup(gathered)
    base = (lax.axis_index("row") * n_col + col) * label_dev
    labels = regroup(doc_labels).T - base

    n_chunk = len(CHUNK_ROWS)
    starts = [sum(CHUNK_ROWS[:k]) for k in range(n_chunk)]
    came = [[None, None] for _ in CHUNK_ROWS]
    lows = [[None, None] for _ in CHUNK_ROWS]
    ends = [[None, None] for _ in CHUNK_ROWS]

    def send(k):
        for half in range(2):
            after = [gathered] if (k, half) == (1, 1) else []
            after = after + lows[k - 2] if k >= 2 else after
            out = messages_of(orders[half], msg_src, blocks, tiles,
                        starts[k], CHUNK_ROWS[k], half, after)
            came[k][half] = [out[0]] + [shift(out[j], axes[half][0], j) for j in range(1, RING)]

    def combine(k):
        for half in range(2):
            second = axes[half][1]
            after = [came[k + 1][h][0] for h in range(2)] if k + 1 < n_chunk else []
            low, high = far_sums(half, pos, table, came[k][half],
                              blk_dev, after)
            lows[k][half] = low
            ends[k][half] = (shift(low, second, 1),
                             shift(high, second, -1))

    send(0)
    for k in range(n_chunk):
        if k + 1 < n_chunk:
            send(k + 1)
        combine(k)

    arrive = lax.dynamic_slice_in_dim(table, col * 2 * cap, 2 * cap, 1)
    dst = arrive[:, :cap].reshape(-1)
    cnt = arrive[:, cap:].reshape(-1).astype(F32)
    hot = dst[None, :] == jnp.arange(blk_dev, dtype=jnp.int32)[:, None]
    inv = 1.0 / (float(blk) + jnp.sum(jnp.where(hot, cnt[None, :], 0.0), axis=1))
    group = jnp.where((labels >= 0) & (labels < label_dev), labels // STEP_ROWS, -1).reshape(-1)
    near = jnp.max((group[None, :] == jnp.arange(label_dev // STEP_ROWS)[:, None]).astype(jnp.int32),
                   axis=1)

    carry = None
    for k, row in enumerate(starts):
        sums = []
        for half in range(2):
            second = axes[half][1]
            up, down = near_sums(half, pos, table, came[k][half],
                             *ends[k][half])
            sums.append((shift(up, second, 1),
                         shift(down, second, -1)))
        carry = head(pos, table, inv, near, came[k], sums, blocks, labels, weight, all_docs, carry,
                     row, k == n_chunk - 1, labels_total, float(pos_count))
    hidden, both = carry

    part_of = n_doc // n_col
    part = swap(both.reshape(n_col, part_of, 2 * width), "col")
    part = jnp.sum(part.astype(F32), axis=0)
    part = part + row_shift(part.astype(BF), lambda z, core: (z, 1 - core)).astype(F32)
    sent = part.astype(BF)
    for by in (1, 2, 3):
        part = part + row_shift(sent, lambda z, core: ((z + by) % (n_row // 2), core)).astype(F32)
    part = part.astype(BF)
    own = lax.dynamic_slice_in_dim(part[:, :width], lax.axis_index("row") * share, share, 0)
    own = jnp.pad(own.reshape(share * share, width // share), ((0, part_of - share * share), (0, 0)))
    whole = spread(jnp.concatenate([part[:, width:], own], axis=1), "col", n_col)
    grad_weight = whole[:, :, :width].reshape(n_doc, width)
    grad_docs = whole[:, :share * share, width:].reshape(docs.shape)
    return hidden.reshape(label_dev, width), grad_docs.astype(F32), grad_weight.astype(F32)


def solution(mesh):
    in_specs = (
        P(("row", "col"), None),
        P(("row", "col"), None, None, None),
        P(("row", "col"), None),
        P(("row", "col"), None),
        P(("row", "col"), None),
        P(),
        P("row", None),
        P(),
    )
    out_specs = (P(("row", "col"), None), P("row", None), P())

    return jax.shard_map(
        per_device, mesh=mesh, in_specs=in_specs, out_specs=out_specs, check_vma=False
    )
```

```python
import functools

import jax
import jax.numpy as jnp
from jax import lax
from jax.experimental import pallas as pl
from jax.experimental.pallas import tpu as pltpu
from jax.sharding import PartitionSpec as P


BF = jnp.bfloat16
F32 = jnp.float32
CHUNK_ROWS = (128, 128)
SUM_ROWS = 128
STEP_ROWS = 64
RING = 4


def wrap(i):
    return lax.rem(i + RING, RING)


def shift_pairs(axis, by):
    pairs = []
    for y in range(RING):
        for x in range(RING):
            ty, tx = ((y + by) % RING, x) if axis == "y" else (y, (x + by) % RING)
            pairs.append((y * RING + x, ty * RING + tx))
    return pairs


def shift(v, axis, by):
    return lax.ppermute(v, "col", shift_pairs(axis, by))


def row_shift(v, to):
    pairs = []
    for i in range(lax.axis_size("row")):
        z, core = to(i // 2, i % 2)
        pairs.append((i, z * 2 + core))
    return lax.ppermute(v, "row", pairs)


def message_kernel(order_ref, src_ref, emb_ref, *refs):
    d = pl.program_id(0)
    for j in range(RING):
        tile_ref, out_ref = refs[j], refs[j - RING]
        p = order_ref[j * RING + d]
        for q in range(tile_ref.shape[1]):
            out_ref[0, q] = jnp.dot(
                tile_ref[0, q], emb_ref[src_ref[p, q]], preferred_element_type=F32
            ).astype(BF)


def messages_of(order, src, blocks, tiles, row, rows, half, after):
    _, cap, blk, _ = tiles.shape
    n_blk, _, width = blocks.shape
    at = row // rows
    part = width // 2
    shape = (RING, cap, rows, part)
    return pl.pallas_call(
        message_kernel,
        grid_spec=pltpu.PrefetchScalarGridSpec(
            num_scalar_prefetch=2,
            grid=(RING,),
            in_specs=[
                pl.BlockSpec((n_blk, blk, part), lambda i, o, s: (0, 0, half),
                             pipeline_mode=pl.Buffered(1)),
            ] + [
                pl.BlockSpec((1, cap, rows, blk),
                             lambda i, o, s, j=j: (o[j * RING + i], 0, at, 0))
                for j in range(RING)
            ] + [pl.BlockSpec(memory_space=pl.ANY)] * len(after),
            out_specs=[pl.BlockSpec((1,) + shape[1:], lambda i, o, s: (i, 0, 0, 0))] * RING,
        ),
        out_shape=[jax.ShapeDtypeStruct(shape, BF)] * RING,
    )(order, src, blocks, *[tiles] * RING, *after)


def pair_kernel(shift_by, order0_ref, order1_ref, src_ref, emb_ref, *refs):
    d = pl.program_id(0)
    part = emb_ref.shape[2] // 2
    for half, order_ref in enumerate((order0_ref, order1_ref)):
        tile_ref, out_ref = refs[half], refs[2 + half]
        p = order_ref[shift_by * RING + d]
        for q in range(tile_ref.shape[1]):
            out_ref[0, q] = jnp.dot(
                tile_ref[0, q], emb_ref[src_ref[p, q], :, half * part:(half + 1) * part],
                preferred_element_type=F32,
            ).astype(BF)


def message_pair(orders, src, blocks, tiles, row, rows, by):
    _, cap, blk, _ = tiles.shape
    n_blk, _, width = blocks.shape
    at = row // rows
    shape = (RING, cap, rows, width // 2)
    return pl.pallas_call(
        functools.partial(pair_kernel, by),
        grid_spec=pltpu.PrefetchScalarGridSpec(
            num_scalar_prefetch=3,
            grid=(RING,),
            in_specs=[
                pl.BlockSpec((n_blk, blk, width), lambda i, a, b, s: (0, 0, 0),
                             pipeline_mode=pl.Buffered(1)),
                pl.BlockSpec((1, cap, rows, blk), lambda i, a, b, s: (a[by * RING + i], 0, at, 0)),
                pl.BlockSpec((1, cap, rows, blk), lambda i, a, b, s: (b[by * RING + i], 0, at, 0)),
            ],
            out_specs=[pl.BlockSpec((1,) + shape[1:], lambda i, a, b, s: (i, 0, 0, 0))] * 2,
        ),
        out_shape=[jax.ShapeDtypeStruct(shape, BF)] * 2,
    )(*orders, src, blocks, tiles, tiles)


def add_slots(acc_ref, table_ref, y, x, half, ahead, parts, columns):
    local = table_ref.shape[0] == RING
    n_blk = acc_ref.shape[0]
    cap = parts[0].shape[1]
    for came, ref in enumerate(parts):
        if half == 0:
            s = y * RING + wrap(x - came)
            p = wrap(y + ahead) * RING + x
        else:
            s = wrap(y - came) * RING + x
            p = y * RING + wrap(x + ahead)
        s = came if local else s

        def add(q, carry):
            dst = table_ref[s, p * 2 * cap + q]
            cnt = table_ref[s, p * 2 * cap + cap + q].astype(F32)

            @pl.when(dst < n_blk)
            def _():
                acc_ref[dst, :, columns] = (
                    acc_ref[dst, :, columns] + cnt * ref[0, q].astype(F32)
                )

            return carry

        lax.fori_loop(0, cap, add, 0)


def far_kernel(half, pos_ref, table_ref, *refs):
    parts, (low_ref, high_ref, acc_ref) = refs[:RING], refs[-3:]
    acc_ref[...] = jnp.zeros_like(acc_ref)
    add_slots(acc_ref, table_ref, pos_ref[0], pos_ref[1], half, 2, parts, slice(None))
    n = low_ref.shape[0]
    low_ref[...] = acc_ref[:n].astype(BF)
    high_ref[...] = acc_ref[n:].astype(BF)


def near_kernel(half, pos_ref, table_ref, *refs):
    ones, threes = refs[:RING], refs[RING:2 * RING]
    low_in, high_in, up_ref, down_ref, acc_ref = refs[2 * RING:]
    n = low_in.shape[0]
    acc_ref[:n] = low_in[...].astype(F32)
    acc_ref[n:] = jnp.zeros_like(acc_ref[n:])
    add_slots(acc_ref, table_ref, pos_ref[0], pos_ref[1], half, 1, ones, slice(None))
    up_ref[...] = acc_ref[...].astype(BF)
    acc_ref[:n] = jnp.zeros_like(acc_ref[:n])
    acc_ref[n:] = high_in[...].astype(F32)
    add_slots(acc_ref, table_ref, pos_ref[0], pos_ref[1], half, 3, threes, slice(None))
    down_ref[...] = acc_ref[...].astype(BF)


SMEM = pl.BlockSpec(memory_space=pltpu.SMEM)


def slot_spec(part, step_rows, ahead):
    return pl.BlockSpec((1, part.shape[1], step_rows, part.shape[3]),
                        lambda i: (ahead, 0, i, 0))


def far_sums(half, pos, table, parts, n_blk, after):
    _, _, rows, cols = parts[0].shape
    step_rows = min(SUM_ROWS, rows)
    n = n_blk // 2
    return pl.pallas_call(
        functools.partial(far_kernel, half),
        grid=(rows // step_rows,),
        in_specs=[SMEM, SMEM] + [slot_spec(a, step_rows, 2) for a in parts]
        + [pl.BlockSpec(memory_space=pl.ANY)] * len(after),
        out_specs=[pl.BlockSpec((n, step_rows, cols), lambda i: (0, i, 0))] * 2,
        out_shape=[jax.ShapeDtypeStruct((n, rows, cols), BF)] * 2,
        scratch_shapes=[pltpu.VMEM((n_blk, step_rows, cols), F32)],
    )(pos, table, *parts, *after)


def near_sums(half, pos, table, parts, low, high):
    _, _, rows, cols = parts[0].shape
    step_rows = min(SUM_ROWS, rows)
    n = low.shape[0]
    rowed = lambda k: pl.BlockSpec((k, step_rows, cols), lambda i: (0, i, 0))
    return pl.pallas_call(
        functools.partial(near_kernel, half),
        grid=(rows // step_rows,),
        in_specs=[SMEM, SMEM] + [slot_spec(a, step_rows, 1) for a in parts]
        + [slot_spec(a, step_rows, 3) for a in parts] + [rowed(n), rowed(n)],
        out_specs=[rowed(2 * n)] * 2,
        out_shape=[jax.ShapeDtypeStruct((2 * n, rows, cols), BF)] * 2,
        scratch_shapes=[pltpu.VMEM((2 * n, step_rows, cols), F32)],
    )(pos, table, *parts, *parts, low, high)


def sigmoid(v):
    return 0.5 * jnp.tanh(0.5 * v) + 0.5


def head_kernel(first, last, row, blk, labels_total, pos_count,
                pos_ref, table_ref, inv_ref, near_ref, *refs):
    mine = (refs[:RING], refs[RING:2 * RING])
    refs = refs[2 * RING:]
    sums = (refs[:2], refs[2:4])
    emb_ref, labels_ref, w_ref, docs_ref = refs[4:8]
    rest = refs[8:]
    if not first:
        gd_in, gw_in, _ = rest[:3]
        rest = rest[3:]
    if last:
        hid_ref, both_ref, acc_ref, agg_ref, ds_ref, prob_ref, gd_ref, gw_ref = rest
    else:
        hid_ref, gd_ref, gw_ref, acc_ref, agg_ref, ds_ref, prob_ref = rest
    step = pl.program_id(0)

    @pl.when(step == 0)
    def _():
        if first:
            gd_ref[...] = jnp.zeros_like(gd_ref)
            gw_ref[...] = jnp.zeros_like(gw_ref)
        else:
            gd_ref[...] = gd_in[...]
            gw_ref[...] = gw_in[...]

    n_blk, rows, width = emb_ref.shape
    part = width // 2
    for half in range(2):
        columns = slice(half * part, (half + 1) * part)
        up, down = sums[half]
        for b in range(n_blk):
            acc_ref[b, :, columns] = (
                float(blk) * emb_ref[b, :, columns].astype(F32)
                + up[b].astype(F32) + down[b].astype(F32)
            )
        add_slots(acc_ref, table_ref, pos_ref[0], pos_ref[1], half, 0, mine[half], columns)
    for b in range(n_blk):
        agg_ref[b * rows:(b + 1) * rows, :] = (acc_ref[b] * inv_ref[b]).astype(BF)
    agg = agg_ref[...]
    pre = jnp.dot(agg, w_ref[...], preferred_element_type=F32)
    sig = sigmoid(pre)
    hid = (pre * sig).astype(BF)
    for b in range(n_blk):
        hid_ref[b] = hid[b * rows:(b + 1) * rows, :]
    scores = lax.dot_general(hid, docs_ref[...], (((1,), (1,)), ((), ())),
                             preferred_element_type=F32)
    prob = sigmoid(scores)
    prob_ref[...] = prob
    ds_ref[...] = (prob * (1.0 / labels_total)).astype(BF)

    def mark(b, carry):
        @pl.when(near_ref[b * (blk // rows) + row // rows + step] > 0)
        def _():
            here = pl.ds(pl.multiple_of(b * rows, rows), rows)
            one = prob_ref[here, :]
            ids = b * blk + row + step * rows + lax.broadcasted_iota(jnp.int32, one.shape, 0)
            hit = labels_ref[0:1, :] == ids
            for j in range(1, labels_ref.shape[0]):
                hit = hit | (labels_ref[j:j + 1, :] == ids)
            ds_ref[here, :] = jnp.where(
                hit, (one - 1.0) * (1.0 / pos_count), one * (1.0 / labels_total)
            ).astype(BF)

        return carry

    lax.fori_loop(0, n_blk, mark, 0)
    ds = ds_ref[...]
    gd_ref[...] += lax.dot_general(ds, hid, (((0,), (0,)), ((), ())),
                                   preferred_element_type=F32)
    dhid = jnp.dot(ds, docs_ref[...], preferred_element_type=F32)
    dpre = (dhid * sig * (1.0 + pre * (1.0 - sig))).astype(BF)
    gw_ref[...] += lax.dot_general(agg, dpre, (((0,), (0,)), ((), ())),
                                   preferred_element_type=F32)
    if last:
        @pl.when(step == pl.num_programs(0) - 1)
        def _():
            both_ref[:, :width] = gd_ref[...].astype(BF)
            both_ref[:, width:] = gw_ref[...].astype(BF)


def head(pos, table, inv, near, mine, sums, blocks, labels, weight, docs, carry, row,
         last, labels_total, pos_count):
    n_blk, blk, width = blocks.shape
    rows = mine[0][0].shape[2]
    step_rows = min(STEP_ROWS, rows)
    at = row // step_rows
    n_doc = docs.shape[0]
    first = carry is None
    full = lambda a: pl.BlockSpec(a, lambda i: (0, 0), pipeline_mode=pl.Buffered(1))
    rowed = lambda n: pl.BlockSpec((n_blk, step_rows, n), lambda i: (0, at + i, 0))
    in_specs = [SMEM, SMEM, SMEM, SMEM]
    args = [pos, table, inv, near]
    for group in mine:
        in_specs += [slot_spec(a, step_rows, 0) for a in group]
        args += list(group)
    for group in sums:
        in_specs += [pl.BlockSpec((n_blk, step_rows, width // 2), lambda i: (0, i, 0))] * 2
        args += list(group)
    in_specs += [rowed(width), full(labels.shape), full(weight.shape), full(docs.shape)]
    args += [blocks, labels, weight, docs]
    aliases = {}
    if not first:
        hid, gd, gw = carry
        in_specs += [full(gd.shape), full(gw.shape), pl.BlockSpec(memory_space=pl.ANY)]
        aliases = {len(args) + 2: 0}
        args += [gd, gw, hid]
    grads = [((n_doc, 2 * width), BF)] if last else [((n_doc, width), F32), ((width, width), F32)]
    return pl.pallas_call(
        functools.partial(head_kernel, first, last, row, blk, labels_total, pos_count),
        grid=(rows // step_rows,),
        in_specs=in_specs,
        out_specs=[rowed(width)] + [pl.BlockSpec(a, lambda i: (0, 0)) for a, _ in grads],
        out_shape=[jax.ShapeDtypeStruct(blocks.shape, BF)]
        + [jax.ShapeDtypeStruct(a, t) for a, t in grads],
        scratch_shapes=[pltpu.VMEM((n_blk, step_rows, width), F32),
                        pltpu.VMEM((n_blk * step_rows, width), BF),
                        pltpu.VMEM((n_blk * step_rows, n_doc), BF),
                        pltpu.VMEM((n_blk * step_rows, n_doc), F32)]
        + ([pltpu.VMEM((n_doc, width), F32), pltpu.VMEM((width, width), F32)] if last else []),
        input_output_aliases=aliases,
        compiler_params=pltpu.CompilerParams(vmem_limit_bytes=48 << 20),
    )(*args)


def swap(x, axis):
    return lax.all_to_all(x, axis, split_axis=0, concat_axis=0, tiled=True)


def spread(x, axis, n):
    return swap(jnp.broadcast_to(x[None], (n,) + x.shape), axis)


def per_device(emb, tiles, msg_src, msg_dst, msg_count, weight, docs, doc_labels):
    n_col = lax.axis_size("col")
    n_row = lax.axis_size("row")
    label_dev, width = emb.shape
    n_peer, cap, blk, _ = tiles.shape
    blk_dev = label_dev // blk
    labels_total = float(label_dev * n_row * n_col)
    pos_count = doc_labels.shape[1]
    n_doc = docs.shape[0] * n_row
    blocks = emb.reshape(blk_dev, blk, width)
    col = lax.axis_index("col")
    y, x = col // RING, col % RING
    pos = jnp.stack([y, x]).astype(jnp.int32)
    steps = jnp.arange(n_peer, dtype=jnp.int32)
    outer, inner = steps // RING, steps % RING
    orders = (wrap(y + inner) * RING + wrap(x + outer), wrap(y + outer) * RING + wrap(x + inner))
    axes = (("x", "y"), ("y", "x"))

    own_table = jnp.concatenate([msg_dst, msg_count], axis=1).reshape(1, -1)
    near_table = jnp.concatenate([own_table] + [shift(own_table, "x", j) for j in range(1, RING)])
    table = own_table.reshape(-1)
    table = spread(table, "col", n_col).reshape(n_col, n_col * 2 * cap)
    share = docs.shape[0] // n_col
    regroup = lambda a: a.reshape((n_row, n_col, share) + a.shape[1:]).swapaxes(0, 1).reshape(a.shape)
    gathered = spread(docs, "row", n_row).reshape(n_doc, width)
    all_docs = regroup(gathered)
    base = (lax.axis_index("row") * n_col + col) * label_dev
    labels = regroup(doc_labels).T - base

    n_chunk = len(CHUNK_ROWS)
    starts = [sum(CHUNK_ROWS[:k]) for k in range(n_chunk)]
    came = [[None, None] for _ in CHUNK_ROWS]
    lows = [[None, None] for _ in CHUNK_ROWS]
    ends = [[None, None] for _ in CHUNK_ROWS]

    def send_first():
        came[0] = [[None] * RING, [None] * RING]
        for j in (1, 3, 2, 0):
            out = message_pair(orders, msg_src, blocks, tiles,
                        starts[0], CHUNK_ROWS[0], j)
            for half in range(2):
                came[0][half][j] = shift(out[half], axes[half][0], j) if j else out[half]

    def send(k):
        for half in range(2):
            out = messages_of(orders[half], msg_src, blocks, tiles,
                        starts[k], CHUNK_ROWS[k], half, [came[0][0][0]])
            came[k][half] = [out[0]] + [shift(out[j], axes[half][0], j) for j in range(1, RING)]

    def combine(k):
        for half in range(2):
            second = axes[half][1]
            after = [came[k + 1][h][0] for h in range(2)] if k + 1 < n_chunk else []
            rows_of = near_table if (k, half) == (0, 0) else table
            low, high = far_sums(half, pos, rows_of, came[k][half],
                              blk_dev, after)
            lows[k][half] = low
            ends[k][half] = (shift(low, second, 1),
                             shift(high, second, -1))

    send_first()
    for k in range(n_chunk):
        if k + 1 < n_chunk:
            send(k + 1)
        combine(k)

    arrive = lax.dynamic_slice_in_dim(table, col * 2 * cap, 2 * cap, 1)
    dst = arrive[:, :cap].reshape(-1)
    cnt = arrive[:, cap:].reshape(-1).astype(F32)
    hot = dst[None, :] == jnp.arange(blk_dev, dtype=jnp.int32)[:, None]
    inv = 1.0 / (float(blk) + jnp.sum(jnp.where(hot, cnt[None, :], 0.0), axis=1))
    group = jnp.where((labels >= 0) & (labels < label_dev), labels // STEP_ROWS, -1).reshape(-1)
    near = jnp.max((group[None, :] == jnp.arange(label_dev // STEP_ROWS)[:, None]).astype(jnp.int32),
                   axis=1)

    carry = None
    for k, row in enumerate(starts):
        sums = []
        for half in range(2):
            second = axes[half][1]
            up, down = near_sums(half, pos, table, came[k][half],
                             *ends[k][half])
            sums.append((shift(up, second, 1),
                         shift(down, second, -1)))
        carry = head(pos, table, inv, near, came[k], sums, blocks, labels, weight, all_docs, carry,
                     row, k == n_chunk - 1, labels_total, float(pos_count))
    hidden, both = carry

    part_of = n_doc // n_col
    part = swap(both.reshape(n_col, part_of, 2 * width), "col")
    part = jnp.sum(part.astype(F32), axis=0)
    part = part + row_shift(part.astype(BF), lambda z, core: (z, 1 - core)).astype(F32)
    sent = part.astype(BF)
    for by in (1, 2, 3):
        part = part + row_shift(sent, lambda z, core: ((z + by) % (n_row // 2), core)).astype(F32)
    part = part.astype(BF)
    own = lax.dynamic_slice_in_dim(part[:, :width], lax.axis_index("row") * share, share, 0)
    own = jnp.pad(own.reshape(share * share, width // share), ((0, part_of - share * share), (0, 0)))
    whole = spread(jnp.concatenate([part[:, width:], own], axis=1), "col", n_col)
    grad_weight = whole[:, :, :width].reshape(n_doc, width)
    grad_docs = whole[:, :share * share, width:].reshape(docs.shape)
    return hidden.reshape(label_dev, width), grad_docs.astype(F32), grad_weight.astype(F32)


def solution(mesh):
    in_specs = (
        P(("row", "col"), None),
        P(("row", "col"), None, None, None),
        P(("row", "col"), None),
        P(("row", "col"), None),
        P(("row", "col"), None),
        P(),
        P("row", None),
        P(),
    )
    out_specs = (P(("row", "col"), None), P("row", None), P())

    return jax.shard_map(
        per_device, mesh=mesh, in_specs=in_specs, out_specs=out_specs, check_vma=False
    )
```

```python
import functools

import jax
import jax.numpy as jnp
from jax import lax
from jax.experimental import pallas as pl
from jax.experimental.pallas import tpu as pltpu
from jax.sharding import PartitionSpec as P


BF = jnp.bfloat16
F32 = jnp.float32
CHUNK_ROWS = (128, 128)
SUM_ROWS = 128
STEP_ROWS = 64
RING = 4


def wrap(i):
    return lax.rem(i + RING, RING)


def shift_pairs(axis, by):
    pairs = []
    for y in range(RING):
        for x in range(RING):
            ty, tx = ((y + by) % RING, x) if axis == "y" else (y, (x + by) % RING)
            pairs.append((y * RING + x, ty * RING + tx))
    return pairs


def shift(v, axis, by):
    return lax.ppermute(v, "col", shift_pairs(axis, by))


def row_shift(v, to):
    pairs = []
    for i in range(lax.axis_size("row")):
        z, core = to(i // 2, i % 2)
        pairs.append((i, z * 2 + core))
    return lax.ppermute(v, "row", pairs)


def message_kernel(order_ref, src_ref, emb_ref, *refs):
    d = pl.program_id(0)
    for j in range(RING):
        tile_ref, out_ref = refs[j], refs[j - RING]
        p = order_ref[j * RING + d]
        for q in range(tile_ref.shape[1]):
            out_ref[0, q] = jnp.dot(
                tile_ref[0, q], emb_ref[src_ref[p, q]], preferred_element_type=F32
            ).astype(BF)


def messages_of(order, src, blocks, tiles, row, rows, half, after):
    _, cap, blk, _ = tiles.shape
    n_blk, _, width = blocks.shape
    at = row // rows
    part = width // 2
    shape = (RING, cap, rows, part)
    return pl.pallas_call(
        message_kernel,
        grid_spec=pltpu.PrefetchScalarGridSpec(
            num_scalar_prefetch=2,
            grid=(RING,),
            in_specs=[
                pl.BlockSpec((n_blk, blk, part), lambda i, o, s: (0, 0, half),
                             pipeline_mode=pl.Buffered(1)),
            ] + [
                pl.BlockSpec((1, cap, rows, blk),
                             lambda i, o, s, j=j: (o[j * RING + i], 0, at, 0))
                for j in range(RING)
            ] + [pl.BlockSpec(memory_space=pl.ANY)] * len(after),
            out_specs=[pl.BlockSpec((1,) + shape[1:], lambda i, o, s: (i, 0, 0, 0))] * RING,
        ),
        out_shape=[jax.ShapeDtypeStruct(shape, BF)] * RING,
    )(order, src, blocks, *[tiles] * RING, *after)


def add_slots(acc_ref, table_ref, y, x, half, ahead, parts, columns):
    local = table_ref.shape[0] == RING
    n_blk = acc_ref.shape[0]
    cap = parts[0].shape[1]
    for came, ref in enumerate(parts):
        if half == 0:
            s = y * RING + wrap(x - came)
            p = wrap(y + ahead) * RING + x
        else:
            s = wrap(y - came) * RING + x
            p = y * RING + wrap(x + ahead)
        s = came if local else s

        def add(q, carry):
            dst = table_ref[s, p * 2 * cap + q]
            cnt = table_ref[s, p * 2 * cap + cap + q].astype(F32)

            @pl.when(dst < n_blk)
            def _():
                acc_ref[dst, :, columns] = (
                    acc_ref[dst, :, columns] + cnt * ref[0, q].astype(F32)
                )

            return carry

        lax.fori_loop(0, cap, add, 0, unroll=columns == slice(None))


def far_kernel(half, pos_ref, table_ref, *refs):
    parts, (low_ref, high_ref, acc_ref) = refs[:RING], refs[-3:]
    acc_ref[...] = jnp.zeros_like(acc_ref)
    add_slots(acc_ref, table_ref, pos_ref[0], pos_ref[1], half, 2, parts, slice(None))
    n = low_ref.shape[0]
    low_ref[...] = acc_ref[:n].astype(BF)
    high_ref[...] = acc_ref[n:].astype(BF)


def near_kernel(half, pos_ref, table_ref, *refs):
    ones, threes = refs[:RING], refs[RING:2 * RING]
    low_in, high_in, up_ref, down_ref, acc_ref = refs[2 * RING:]
    n = low_in.shape[0]
    acc_ref[:n] = low_in[...].astype(F32)
    acc_ref[n:] = jnp.zeros_like(acc_ref[n:])
    add_slots(acc_ref, table_ref, pos_ref[0], pos_ref[1], half, 1, ones, slice(None))
    up_ref[...] = acc_ref[...].astype(BF)
    acc_ref[:n] = jnp.zeros_like(acc_ref[:n])
    acc_ref[n:] = high_in[...].astype(F32)
    add_slots(acc_ref, table_ref, pos_ref[0], pos_ref[1], half, 3, threes, slice(None))
    down_ref[...] = acc_ref[...].astype(BF)


SMEM = pl.BlockSpec(memory_space=pltpu.SMEM)


def slot_spec(part, step_rows, ahead):
    return pl.BlockSpec((1, part.shape[1], step_rows, part.shape[3]),
                        lambda i: (ahead, 0, i, 0))


def far_sums(half, pos, table, parts, n_blk, after):
    _, _, rows, cols = parts[0].shape
    step_rows = min(SUM_ROWS, rows)
    n = n_blk // 2
    return pl.pallas_call(
        functools.partial(far_kernel, half),
        grid=(rows // step_rows,),
        in_specs=[SMEM, SMEM] + [slot_spec(a, step_rows, 2) for a in parts]
        + [pl.BlockSpec(memory_space=pl.ANY)] * len(after),
        out_specs=[pl.BlockSpec((n, step_rows, cols), lambda i: (0, i, 0))] * 2,
        out_shape=[jax.ShapeDtypeStruct((n, rows, cols), BF)] * 2,
        scratch_shapes=[pltpu.VMEM((n_blk, step_rows, cols), F32)],
    )(pos, table, *parts, *after)


def near_sums(half, pos, table, parts, low, high):
    _, _, rows, cols = parts[0].shape
    step_rows = min(SUM_ROWS, rows)
    n = low.shape[0]
    rowed = lambda k: pl.BlockSpec((k, step_rows, cols), lambda i: (0, i, 0))
    return pl.pallas_call(
        functools.partial(near_kernel, half),
        grid=(rows // step_rows,),
        in_specs=[SMEM, SMEM] + [slot_spec(a, step_rows, 1) for a in parts]
        + [slot_spec(a, step_rows, 3) for a in parts] + [rowed(n), rowed(n)],
        out_specs=[rowed(2 * n)] * 2,
        out_shape=[jax.ShapeDtypeStruct((2 * n, rows, cols), BF)] * 2,
        scratch_shapes=[pltpu.VMEM((2 * n, step_rows, cols), F32)],
    )(pos, table, *parts, *parts, low, high)


def sigmoid(v):
    return 0.5 * jnp.tanh(0.5 * v) + 0.5


def head_kernel(first, last, row, blk, labels_total, pos_count,
                pos_ref, table_ref, inv_ref, near_ref, *refs):
    mine = (refs[:RING], refs[RING:2 * RING])
    refs = refs[2 * RING:]
    sums = (refs[:2], refs[2:4])
    emb_ref, labels_ref, w_ref, docs_ref = refs[4:8]
    rest = refs[8:]
    if not first:
        gd_in, gw_in, _ = rest[:3]
        rest = rest[3:]
    if last:
        hid_ref, both_ref, acc_ref, agg_ref, ds_ref, prob_ref, gd_ref, gw_ref = rest
    else:
        hid_ref, gd_ref, gw_ref, acc_ref, agg_ref, ds_ref, prob_ref = rest
    step = pl.program_id(0)

    @pl.when(step == 0)
    def _():
        if first:
            gd_ref[...] = jnp.zeros_like(gd_ref)
            gw_ref[...] = jnp.zeros_like(gw_ref)
        else:
            gd_ref[...] = gd_in[...]
            gw_ref[...] = gw_in[...]

    n_blk, rows, width = emb_ref.shape
    part = width // 2
    for half in range(2):
        columns = slice(half * part, (half + 1) * part)
        up, down = sums[half]
        for b in range(n_blk):
            acc_ref[b, :, columns] = (
                float(blk) * emb_ref[b, :, columns].astype(F32)
                + up[b].astype(F32) + down[b].astype(F32)
            )
        add_slots(acc_ref, table_ref, pos_ref[0], pos_ref[1], half, 0, mine[half], columns)
    for b in range(n_blk):
        agg_ref[b * rows:(b + 1) * rows, :] = (acc_ref[b] * inv_ref[b]).astype(BF)
    agg = agg_ref[...]
    pre = jnp.dot(agg, w_ref[...], preferred_element_type=F32)
    sig = sigmoid(pre)
    hid = (pre * sig).astype(BF)
    for b in range(n_blk):
        hid_ref[b] = hid[b * rows:(b + 1) * rows, :]
    scores = lax.dot_general(hid, docs_ref[...], (((1,), (1,)), ((), ())),
                             preferred_element_type=F32)
    prob = sigmoid(scores)
    prob_ref[...] = prob
    ds_ref[...] = (prob * (1.0 / labels_total)).astype(BF)

    def mark(b, carry):
        @pl.when(near_ref[b * (blk // rows) + row // rows + step] > 0)
        def _():
            here = pl.ds(pl.multiple_of(b * rows, rows), rows)
            one = prob_ref[here, :]
            ids = b * blk + row + step * rows + lax.broadcasted_iota(jnp.int32, one.shape, 0)
            hit = labels_ref[0:1, :] == ids
            for j in range(1, labels_ref.shape[0]):
                hit = hit | (labels_ref[j:j + 1, :] == ids)
            ds_ref[here, :] = jnp.where(
                hit, (one - 1.0) * (1.0 / pos_count), one * (1.0 / labels_total)
            ).astype(BF)

        return carry

    lax.fori_loop(0, n_blk, mark, 0)
    ds = ds_ref[...]
    gd_ref[...] += lax.dot_general(ds, hid, (((0,), (0,)), ((), ())),
                                   preferred_element_type=F32)
    dhid = jnp.dot(ds, docs_ref[...], preferred_element_type=F32)
    dpre = (dhid * sig * (1.0 + pre * (1.0 - sig))).astype(BF)
    gw_ref[...] += lax.dot_general(agg, dpre, (((0,), (0,)), ((), ())),
                                   preferred_element_type=F32)
    if last:
        @pl.when(step == pl.num_programs(0) - 1)
        def _():
            both_ref[:, :width] = gd_ref[...].astype(BF)
            both_ref[:, width:] = gw_ref[...].astype(BF)


def head(pos, table, inv, near, mine, sums, blocks, labels, weight, docs, carry, row,
         last, labels_total, pos_count):
    n_blk, blk, width = blocks.shape
    rows = mine[0][0].shape[2]
    step_rows = min(STEP_ROWS, rows)
    at = row // step_rows
    n_doc = docs.shape[0]
    first = carry is None
    full = lambda a: pl.BlockSpec(a, lambda i: (0, 0), pipeline_mode=pl.Buffered(1))
    rowed = lambda n: pl.BlockSpec((n_blk, step_rows, n), lambda i: (0, at + i, 0))
    in_specs = [SMEM, SMEM, SMEM, SMEM]
    args = [pos, table, inv, near]
    for group in mine:
        in_specs += [slot_spec(a, step_rows, 0) for a in group]
        args += list(group)
    for group in sums:
        in_specs += [pl.BlockSpec((n_blk, step_rows, width // 2), lambda i: (0, i, 0))] * 2
        args += list(group)
    in_specs += [rowed(width), full(labels.shape), full(weight.shape), full(docs.shape)]
    args += [blocks, labels, weight, docs]
    aliases = {}
    if not first:
        hid, gd, gw = carry
        in_specs += [full(gd.shape), full(gw.shape), pl.BlockSpec(memory_space=pl.ANY)]
        aliases = {len(args) + 2: 0}
        args += [gd, gw, hid]
    grads = [((n_doc, 2 * width), BF)] if last else [((n_doc, width), F32), ((width, width), F32)]
    return pl.pallas_call(
        functools.partial(head_kernel, first, last, row, blk, labels_total, pos_count),
        grid=(rows // step_rows,),
        in_specs=in_specs,
        out_specs=[rowed(width)] + [pl.BlockSpec(a, lambda i: (0, 0)) for a, _ in grads],
        out_shape=[jax.ShapeDtypeStruct(blocks.shape, BF)]
        + [jax.ShapeDtypeStruct(a, t) for a, t in grads],
        scratch_shapes=[pltpu.VMEM((n_blk, step_rows, width), F32),
                        pltpu.VMEM((n_blk * step_rows, width), BF),
                        pltpu.VMEM((n_blk * step_rows, n_doc), BF),
                        pltpu.VMEM((n_blk * step_rows, n_doc), F32)]
        + ([pltpu.VMEM((n_doc, width), F32), pltpu.VMEM((width, width), F32)] if last else []),
        input_output_aliases=aliases,
        compiler_params=pltpu.CompilerParams(vmem_limit_bytes=48 << 20),
    )(*args)


def swap(x, axis):
    return lax.all_to_all(x, axis, split_axis=0, concat_axis=0, tiled=True)


def spread(x, axis, n):
    return swap(jnp.broadcast_to(x[None], (n,) + x.shape), axis)


def per_device(emb, tiles, msg_src, msg_dst, msg_count, weight, docs, doc_labels):
    n_col = lax.axis_size("col")
    n_row = lax.axis_size("row")
    label_dev, width = emb.shape
    n_peer, cap, blk, _ = tiles.shape
    blk_dev = label_dev // blk
    labels_total = float(label_dev * n_row * n_col)
    pos_count = doc_labels.shape[1]
    n_doc = docs.shape[0] * n_row
    blocks = emb.reshape(blk_dev, blk, width)
    col = lax.axis_index("col")
    y, x = col // RING, col % RING
    pos = jnp.stack([y, x]).astype(jnp.int32)
    steps = jnp.arange(n_peer, dtype=jnp.int32)
    outer, inner = steps // RING, steps % RING
    orders = (wrap(y + inner) * RING + wrap(x + outer), wrap(y + outer) * RING + wrap(x + inner))
    axes = (("x", "y"), ("y", "x"))

    own_table = jnp.concatenate([msg_dst, msg_count], axis=1).reshape(1, -1)
    near_table = jnp.concatenate([own_table] + [shift(own_table, "x", j) for j in range(1, RING)])
    table = own_table.reshape(-1)
    table = spread(table, "col", n_col).reshape(n_col, n_col * 2 * cap)
    share = docs.shape[0] // n_col
    regroup = lambda a: a.reshape((n_row, n_col, share) + a.shape[1:]).swapaxes(0, 1).reshape(a.shape)
    gathered = spread(docs, "row", n_row).reshape(n_doc, width)
    all_docs = regroup(gathered)
    base = (lax.axis_index("row") * n_col + col) * label_dev
    labels = regroup(doc_labels).T - base

    n_chunk = len(CHUNK_ROWS)
    starts = [sum(CHUNK_ROWS[:k]) for k in range(n_chunk)]
    came = [[None, None] for _ in CHUNK_ROWS]
    lows = [[None, None] for _ in CHUNK_ROWS]
    ends = [[None, None] for _ in CHUNK_ROWS]

    def send(k):
        for half in range(2):
            after = [gathered] if (k, half) == (1, 1) else []
            after = after + lows[k - 2] if k >= 2 else after
            out = messages_of(orders[half], msg_src, blocks, tiles,
                        starts[k], CHUNK_ROWS[k], half, after)
            came[k][half] = [out[0]] + [shift(out[j], axes[half][0], j) for j in range(1, RING)]

    def combine(k):
        for half in range(2):
            second = axes[half][1]
            after = [came[k + 1][h][0] for h in range(2)] if k + 1 < n_chunk else []
            rows_of = near_table if (k, half) == (0, 0) else table
            low, high = far_sums(half, pos, rows_of, came[k][half],
                              blk_dev, after)
            lows[k][half] = low
            ends[k][half] = (shift(low, second, 1),
                             shift(high, second, -1))

    send(0)
    for k in range(n_chunk):
        if k + 1 < n_chunk:
            send(k + 1)
        combine(k)

    arrive = lax.dynamic_slice_in_dim(table, col * 2 * cap, 2 * cap, 1)
    dst = arrive[:, :cap].reshape(-1)
    cnt = arrive[:, cap:].reshape(-1).astype(F32)
    hot = dst[None, :] == jnp.arange(blk_dev, dtype=jnp.int32)[:, None]
    inv = 1.0 / (float(blk) + jnp.sum(jnp.where(hot, cnt[None, :], 0.0), axis=1))
    group = jnp.where((labels >= 0) & (labels < label_dev), labels // STEP_ROWS, -1).reshape(-1)
    near = jnp.max((group[None, :] == jnp.arange(label_dev // STEP_ROWS)[:, None]).astype(jnp.int32),
                   axis=1)

    carry = None
    for k, row in enumerate(starts):
        sums = []
        for half in range(2):
            second = axes[half][1]
            up, down = near_sums(half, pos, table, came[k][half],
                             *ends[k][half])
            sums.append((shift(up, second, 1),
                         shift(down, second, -1)))
        carry = head(pos, table, inv, near, came[k], sums, blocks, labels, weight, all_docs, carry,
                     row, k == n_chunk - 1, labels_total, float(pos_count))
    hidden, both = carry

    part_of = n_doc // n_col
    part = swap(both.reshape(n_col, part_of, 2 * width), "col")
    part = jnp.sum(part.astype(F32), axis=0)
    part = part + row_shift(part.astype(BF), lambda z, core: (z, 1 - core)).astype(F32)
    sent = part.astype(BF)
    for by in (1, 2, 3):
        part = part + row_shift(sent, lambda z, core: ((z + by) % (n_row // 2), core)).astype(F32)
    part = part.astype(BF)
    own = lax.dynamic_slice_in_dim(part[:, :width], lax.axis_index("row") * share, share, 0)
    own = jnp.pad(own.reshape(share * share, width // share), ((0, part_of - share * share), (0, 0)))
    whole = spread(jnp.concatenate([part[:, width:], own], axis=1), "col", n_col)
    grad_weight = whole[:, :, :width].reshape(n_doc, width)
    grad_docs = whole[:, :share * share, width:].reshape(docs.shape)
    return hidden.reshape(label_dev, width), grad_docs.astype(F32), grad_weight.astype(F32)


def solution(mesh):
    in_specs = (
        P(("row", "col"), None),
        P(("row", "col"), None, None, None),
        P(("row", "col"), None),
        P(("row", "col"), None),
        P(("row", "col"), None),
        P(),
        P("row", None),
        P(),
    )
    out_specs = (P(("row", "col"), None), P("row", None), P())

    return jax.shard_map(
        per_device, mesh=mesh, in_specs=in_specs, out_specs=out_specs, check_vma=False
    )
```
